768 devices in a mesh: depth: 16 (over y_hi, x), height: 12 (over z), filt: 4 (over y_lo, core).
Axes of the slice: x: 4, y: 8 (y_hi: 4, y_lo: 2; y = y_hi * 2 + y_lo), z: 12, core: 2. Of those that a mesh axis runs over, the one named last changes fastest.
Arguments:
- volume: bfloat16 [64, 48, 64, 256], P('depth', 'height', None, 'filt'), may hold values from -6 to 6
- kernel_one: bfloat16 [3, 3, 3, 256, 256], replicated, may hold values from -0.078125 to 0.078125
- bias_one: float32 [256], replicated, may hold values from -3 to 3
- kernel_two: bfloat16 [3, 3, 3, 256, 256], replicated, may hold values from -0.078125 to 0.078125
- bias_two: float32 [256], replicated, may hold values from -3 to 3
Outputs:
- features: bfloat16 [64, 48, 64, 256], P('depth', 'height', None, 'filt')
The draws below stay inside these ranges and needn't reach their ends.
All inputs are finite; a program needn't handle non-finite values.
Results may differ from the reference program's by a relative error of at most 0.0044.
Values may be sent and summed in bfloat16 or wider, within the bound.
A program may use at most 32 MiB of HBM per device.

```python
import jax
import jax.numpy as jnp
from jax import lax

CHANNELS = 256
WID = 64
DEPTH_ALL = 64
HEIGHT_ALL = 48


def steps_of(key, shape, shards, smallest, largest):
    level, own = 1.0, jax.random.fold_in(key, 6)
    for dim, blocks in shards:
        draws = jnp.exp(jax.random.uniform(jax.random.fold_in(own, dim), (blocks,), jnp.float32, smallest / len(shards), largest / len(shards)))
        level = level * jnp.repeat(draws, shape[dim] // blocks).reshape([-1 if axis == dim else 1 for axis in range(len(shape))])
    return level


def centred(stream_key, shape, spread, most, split=(), dtype=jnp.bfloat16):
    array = jax.random.normal(stream_key, shape, jnp.float32) * spread
    if len(split) > 0:
        array = steps_of(stream_key, shape, split, -0.22, 0.18) * array
    return jnp.clip(array, min=-most, max=most).astype(dtype)


def setup_inputs(seed: int = 0) -> dict:
    streams_of = jax.random.split(jax.random.key(seed), 6)
    return {
        "volume": centred(streams_of[0], (DEPTH_ALL, HEIGHT_ALL, WID, CHANNELS), 1.0, 6.0, ((0, 16), (1, 12), (3, 4))),
        "kernel_one": centred(streams_of[1], (3, 3, 3, CHANNELS, CHANNELS), (27 * CHANNELS) ** -0.5, 0.078125),
        "bias_one": centred(streams_of[2], (CHANNELS,), 0.5, 3.0, (), jnp.float32),
        "kernel_two": centred(streams_of[3], (3, 3, 3, CHANNELS, CHANNELS), (27 * CHANNELS) ** -0.5, 0.078125),
        "bias_two": centred(streams_of[4], (CHANNELS,), 0.5, 3.0, (), jnp.float32),
    }


def leaky(value):
    return jnp.where(value > 0, value, 0.3 * value)


def convolve(field, kernel):
    out = lax.conv_general_dilated(field.astype(jnp.float32)[None], kernel.astype(jnp.float32), (1, 1, 1), [(1, 1), (1, 1), (1, 1)], dimension_numbers=("NDHWC", "DHWIO", "NDHWC"), precision=lax.Precision.HIGHEST)
    return out[0]


def reference(volume, kernel_one, bias_one, kernel_two, bias_two):
    hidden = leaky(convolve(volume, kernel_one) + bias_one).astype(jnp.bfloat16)
    return leaky(convolve(hidden, kernel_two) + bias_two).astype(jnp.bfloat16)
```

```python
import functools

import jax
import jax.numpy as jnp
from jax import lax
from jax.experimental import pallas as pl
from jax.experimental.pallas import tpu as pltpu
from jax.sharding import PartitionSpec as P

MESH = pl.DeviceIdType.MESH
DIRS = ((-1, 0), (1, 0), (0, -1), (0, 1), (-1, -1), (-1, 1), (1, -1), (1, 1))


def opposite(k):
    return DIRS.index((-DIRS[k][0], -DIRS[k][1]))


def halo_part(step):
    return pl.ds({-1: 0, 0: 1, 1: 3}[step], 2 if step == 0 else 1)


def edge_part(step):
    return pl.ds({-1: 1, 0: 1, 1: 2}[step], 2 if step == 0 else 1)


def flip_of(d):
    return (d % 2) * (1 - (d % 4) // 2)


def leaky(value):
    return jnp.where(value > 0, value, 0.3 * value)


def convolve(x, w, bias):
    width, chans = x.shape[2], x.shape[3]
    rows = 4 * width
    sums = []
    for c in range(3):
        acc = None
        for a in range(3):
            for b in range(3):
                lhs = x[a : a + 2, b : b + 2].reshape(rows, chans)
                part = jnp.dot(lhs, w[a, b, c], preferred_element_type=jnp.float32)
                acc = part if acc is None else acc + part
        sums.append(acc)
    w_of = lax.rem(lax.broadcasted_iota(jnp.int32, (rows, chans), 0), width)
    low = jnp.where(w_of == 0, 0.0, pltpu.roll(sums[0], 1, 0))
    high = jnp.where(w_of == width - 1, 0.0, pltpu.roll(sums[2], rows - 1, 0))
    total = low + sums[1] + high + bias[...]
    return leaky(total).astype(jnp.bfloat16)


def kernel(
    depths, heights,
    vol, k1, b1, k2, b2, out,
    xv, w1, w2, bb1, bb2, xs, ra, xh, hh, os,
    lsem, sa, qa, sb, qb, sc, qc, se, qe,
):
    d, h, f = lax.axis_index("depth"), lax.axis_index("height"), lax.axis_index("filt")
    flip = flip_of(d)
    fd, fh = (f // 2 + flip) % 2, f % 2
    quarter = 2 * fd + fh
    fine_d, fine_h = 2 * d + fd, 2 * h + fh
    width, shard = vol.shape[2], vol.shape[3]
    rows = 3 - jnp.where(fine_d == 0, 1, 0) - jnp.where(fine_d == 2 * depths - 1, 1, 0)
    columns = 3 - jnp.where(fine_h == 0, 1, 0) - jnp.where(fine_h == 2 * heights - 1, 1, 0)
    peers = rows * columns - 1

    def neighbour(k):
        nd, nh = fine_d + DIRS[k][0], fine_h + DIRS[k][1]
        block = nd // 2
        nf = 2 * ((nd + flip_of(block)) % 2) + nh % 2
        valid = (nd >= 0) & (nd < 2 * depths) & (nh >= 0) & (nh < 2 * heights)
        return valid, {"depth": block, "height": nh // 2, "filt": nf}

    loads = [
        pltpu.make_async_copy(src, dst, lsem.at[i])
        for i, (src, dst) in enumerate(((vol, xv), (b1, bb1), (b2, bb2), (k1, w1), (k2, w2)))
    ]
    for load in loads:
        load.start()

    barrier = pltpu.get_barrier_semaphore()
    for k in range(8):
        valid, device = neighbour(k)

        @pl.when(valid)
        def _():
            pl.semaphore_signal(barrier, inc=1, device_id=device, device_id_type=MESH)

    for k in range(8):
        valid, _ = neighbour(k)

        @pl.when(jnp.logical_not(valid))
        def _():
            part = (halo_part(DIRS[k][0]), halo_part(DIRS[k][1]))
            for ref in (xh, hh):
                ref[part] = jnp.zeros_like(ref[part])

    loads[0].wait()
    for q in range(4):
        top, side = 2 * (q // 2), 2 * (q % 2)
        xs[q] = jnp.concatenate([xv[top : top + 2, side], xv[top : top + 2, side + 1]], axis=-1)

    pl.semaphore_wait(barrier, peers)

    def gather(q):
        return pltpu.make_async_remote_copy(
            src_ref=xs.at[q], dst_ref=ra.at[f], send_sem=sa.at[q], recv_sem=qa.at[f],
            device_id={"filt": 2 * ((q // 2 + flip) % 2) + q % 2}, device_id_type=MESH)

    for q in range(4):
        @pl.when(q != quarter)
        def _():
            gather(q).start()

    ra[f] = xs[quarter]
    for g in range(4):
        @pl.when(g != f)
        def _():
            pltpu.make_async_remote_copy(
                src_ref=xs.at[0], dst_ref=ra.at[g], send_sem=sa.at[0], recv_sem=qa.at[g],
                device_id={"filt": g}, device_id_type=MESH).wait_recv()

    for i in range(2):
        for j in range(2):
            xh[1 + i, 1 + j] = jnp.concatenate(
                [ra[g, i, :, j * shard : (j + 1) * shard] for g in range(4)], axis=-1)

    def halo(ref, send, recv, k):
        valid, device = neighbour(k)
        sd, sh = DIRS[k]
        edge = ref.at[edge_part(sd), edge_part(sh)]

        def copy():
            return pltpu.make_async_remote_copy(
                src_ref=edge, dst_ref=ref.at[halo_part(-sd), halo_part(-sh)],
                send_sem=send.at[k], recv_sem=recv.at[opposite(k)],
                device_id=device, device_id_type=MESH)

        def arrival():
            return pltpu.make_async_remote_copy(
                src_ref=edge, dst_ref=ref.at[halo_part(sd), halo_part(sh)],
                send_sem=send.at[k], recv_sem=recv.at[k],
                device_id=device, device_id_type=MESH)

        return valid, copy, arrival

    def exchange(ref, send, recv):
        for k in reversed(range(8)):
            valid, copy, _ = halo(ref, send, recv, k)

            @pl.when(valid)
            def _():
                copy().start()

        for k in range(8):
            valid, _, arrival = halo(ref, send, recv, k)

            @pl.when(valid)
            def _():
                arrival().wait_recv()

    exchange(xh, sb, qb)
    loads[1].wait()
    loads[3].wait()
    hidden = convolve(xh, w1, bb1)
    hh[1:3, 1:3] = hidden.reshape(2, 2, width, 4 * shard)

    exchange(hh, sc, qc)
    loads[2].wait()
    loads[4].wait()
    result = convolve(hh, w2, bb2).reshape(2, 2, width, 4 * shard)
    for g in range(4):
        part = result[:, :, :, g * shard : (g + 1) * shard]
        os[g] = jnp.concatenate([part[:, 0], part[:, 1]], axis=-1)

    def scatter(g):
        return pltpu.make_async_remote_copy(
            src_ref=os.at[g], dst_ref=out.at[quarter], send_sem=se.at[g], recv_sem=qe.at[quarter],
            device_id={"filt": g}, device_id_type=MESH)

    for g in range(4):
        @pl.when(g != f)
        def _():
            scatter(g).start()

    own = pltpu.make_async_copy(os.at[f], out.at[quarter], lsem.at[5])
    own.start()
    own.wait()
    for q in range(4):
        @pl.when(q != quarter)
        def _():
            pltpu.make_async_remote_copy(
                src_ref=os.at[0], dst_ref=out.at[q], send_sem=se.at[0], recv_sem=qe.at[q],
                device_id={"filt": 2 * ((q // 2 + flip) % 2) + q % 2}, device_id_type=MESH).wait_recv()

    for q in range(4):
        @pl.when(q != quarter)
        def _():
            gather(q).wait_send()

        @pl.when(q != f)
        def _():
            scatter(q).wait_send()

    for k in range(8):
        valid, first, _ = halo(xh, sb, qb, k)
        _, second, _ = halo(hh, sc, qc, k)

        @pl.when(valid)
        def _():
            first().wait_send()
            second().wait_send()


def body(depths, heights, volume, kernel_one, bias_one, kernel_two, bias_two):
    _, _, width, shard = volume.shape
    chans = 4 * shard
    bf16, dma = jnp.bfloat16, pltpu.SemaphoreType.DMA
    packed = pltpu.VMEM((4, 2, width, 2 * shard), bf16)
    parts = pl.pallas_call(
        functools.partial(kernel, depths, heights),
        out_shape=jax.ShapeDtypeStruct((4, 2, width, 2 * shard), bf16),
        in_specs=[pl.BlockSpec(memory_space=pltpu.HBM)] * 5,
        out_specs=pl.BlockSpec(memory_space=pl.ANY),
        scratch_shapes=[
            pltpu.VMEM(volume.shape, bf16),
            pltpu.VMEM(kernel_one.shape, bf16),
            pltpu.VMEM(kernel_two.shape, bf16),
            pltpu.VMEM((1, chans), jnp.float32),
            pltpu.VMEM((1, chans), jnp.float32),
            packed,
            packed,
            pltpu.VMEM((4, 4, width, chans), bf16),
            pltpu.VMEM((4, 4, width, chans), bf16),
            packed,
            dma((6,)), dma((4,)), dma((4,)), dma((8,)), dma((8,)), dma((8,)), dma((8,)), dma((4,)), dma((4,)),
        ],
        compiler_params=pltpu.CompilerParams(
            collective_id=0, has_side_effects=True, vmem_limit_bytes=67_043_328),
    )(volume, kernel_one, bias_one.reshape(1, chans), kernel_two, bias_two.reshape(1, chans))
    parts = parts.reshape(2, 2, 2, width, 2, shard)
    return parts.transpose(0, 2, 1, 4, 3, 5).reshape(4, 4, width, shard)


def solution(mesh):
    in_specs = (P("depth", "height", None, "filt"), P(), P(), P(), P())
    out_specs = P("depth", "height", None, "filt")
    step = functools.partial(body, mesh.shape["depth"], mesh.shape["height"])
    return jax.shard_map(step, mesh=mesh, in_specs=in_specs, out_specs=out_specs, check_vma=False)
```

```python
import functools

import jax
import jax.numpy as jnp
from jax import lax
from jax.experimental import pallas as pl
from jax.experimental.pallas import tpu as pltpu
from jax.sharding import PartitionSpec as P

MESH = pl.DeviceIdType.MESH
VMEM_LIMIT = 67_043_328
MESSAGES = (
    (0, -1, 1), (0, 1, 1), (0, -1, 2), (0, 1, 2),
    (-1, -1, 1), (-1, 1, 1), (-1, 0, 1),
    (1, -1, 2), (1, 1, 2), (1, 0, 2),
)
SIDES, UPPER, LOWER = (0, 1, 2, 3), (4, 5, 6), (7, 8, 9)
STEPS = tuple((a, b) for a in (-1, 0, 1) for b in (-1, 0, 1) if (a, b) != (0, 0))


def opposite(m):
    sd, sh, row = MESSAGES[m]
    return MESSAGES.index((-sd, -sh, row if sd == 0 else 3 - row))


def edge_of(m):
    sd, sh, row = MESSAGES[m]
    return pl.ds(row, 1), pl.ds(1 if sh <= 0 else 2, 2 if sh == 0 else 1)


def halo_of(m):
    sd, sh, row = MESSAGES[m]
    return pl.ds({-1: 0, 0: row, 1: 3}[sd], 1), pl.ds({-1: 0, 0: 1, 1: 3}[sh], 2 if sh == 0 else 1)


def flip_of(d):
    return (d % 2) * (1 - (d % 4) // 2)


def leaky(value):
    return jnp.where(value > 0, value, 0.3 * value)


def taps(x, w, rows, count, a, c):
    width, chans = x.shape[2], x.shape[3]
    total = None
    for b in range(3):
        lhs = x[rows : rows + count, b : b + 2].reshape(count * 2 * width, chans)
        part = jnp.dot(lhs, w[a, b, c], preferred_element_type=jnp.float32)
        total = part if total is None else total + part
    return total


def inner_taps(x, w, acc):
    half = 2 * x.shape[2]
    for c in range(3):
        both = taps(x, w, 1, 2, 1, c)
        acc[c, 0] = both[:half] + taps(x, w, 2, 1, 2, c)
        acc[c, 1] = both[half:] + taps(x, w, 1, 1, 0, c)


def outer_taps(x, w, acc, bias, row):
    width, chans = x.shape[2], x.shape[3]
    rows = 2 * width
    low, centre, high = (acc[c, row] + taps(x, w, 3 * row, 1, 2 * row, c) for c in range(3))
    w_of = lax.rem(lax.broadcasted_iota(jnp.int32, (rows, chans), 0), width)
    low = jnp.where(w_of == 0, 0.0, pltpu.roll(low, 1, 0))
    high = jnp.where(w_of == width - 1, 0.0, pltpu.roll(high, rows - 1, 0))
    return leaky(low + centre + high + bias[...]).astype(jnp.bfloat16)


def kernel(
    depths, heights,
    vol, k1, b1, k2, b2, out,
    xv, w1, w2, bb1, bb2, xs, ra, xh, hh, os, ro, acc,
    lsem, sa, qa, sb, qb, sc, qc, se, qe,
):
    d, h, f = lax.axis_index("depth"), lax.axis_index("height"), lax.axis_index("filt")
    flip = flip_of(d)
    width, shard = vol.shape[2], vol.shape[3]

    def quarter_of(g):
        return 2 * ((g // 2 + flip) % 2) + g % 2

    quarter = quarter_of(f)
    peers = [(f + r) % 4 for r in (2, 3, 1)]
    fine_d, fine_h = 2 * d + quarter // 2, 2 * h + f % 2
    has = {
        -1: (fine_d > 0, fine_h > 0),
        0: (True, True),
        1: (fine_d < 2 * depths - 1, fine_h < 2 * heights - 1),
    }

    def neighbour(sd, sh):
        nd, nh = fine_d + sd, fine_h + sh
        block = nd // 2
        nf = 2 * ((nd + flip_of(block)) % 2) + nh % 2
        if sd == 0:
            valid = has[sh][1]
        else:
            valid = has[sd][0] if sh == 0 else has[sd][0] & has[sh][1]
        return valid, {"depth": block, "height": nh // 2, "filt": nf}

    loads = [
        pltpu.make_async_copy(src, dst, lsem.at[i])
        for i, (src, dst) in enumerate(((vol, xv), (b1, bb1), (b2, bb2), (k1, w1), (k2, w2)))
    ]
    loads[0].start()
    barrier = pltpu.get_barrier_semaphore()
    for step in STEPS:
        valid, device = neighbour(*step)

        @pl.when(valid)
        def _():
            pl.semaphore_signal(barrier, inc=1, device_id=device, device_id_type=MESH)

    for load in loads[1:]:
        load.start()
    loads[0].wait()
    for q in range(4):
        top, side = 2 * (q // 2), 2 * (q % 2)
        xs[q] = jnp.concatenate([xv[top : top + 2, side], xv[top : top + 2, side + 1]], axis=-1)

    for m in range(len(MESSAGES)):
        valid, _ = neighbour(*MESSAGES[m][:2])

        @pl.when(jnp.logical_not(valid))
        def _():
            for ref in (xh, hh):
                ref[halo_of(m)] = jnp.zeros_like(ref[halo_of(m)])

    tall = 3 - jnp.where(fine_d == 0, 1, 0) - jnp.where(fine_d == 2 * depths - 1, 1, 0)
    wide = 3 - jnp.where(fine_h == 0, 1, 0) - jnp.where(fine_h == 2 * heights - 1, 1, 0)
    pl.semaphore_wait(barrier, tall * wide - 1)

    def gather(g):
        return pltpu.make_async_remote_copy(
            src_ref=xs.at[quarter_of(g)], dst_ref=ra.at[f], send_sem=sa.at[g], recv_sem=qa.at[f],
            device_id={"filt": g}, device_id_type=MESH)

    def gathered(g):
        return pltpu.make_async_remote_copy(
            src_ref=xs.at[quarter], dst_ref=ra.at[g], send_sem=sa.at[g], recv_sem=qa.at[g],
            device_id={"filt": g}, device_id_type=MESH)

    for g in peers:
        gather(g).start()
    ra[f] = xs[quarter]
    for g in reversed(peers):
        gathered(g).wait_recv()
    for i in range(2):
        for j in range(2):
            xh[1 + i, 1 + j] = jnp.concatenate(
                [ra[g, i, :, j * shard : (j + 1) * shard] for g in range(4)], axis=-1)

    def halo(ref, send, recv, m):
        valid, device = neighbour(*MESSAGES[m][:2])

        def copy():
            return pltpu.make_async_remote_copy(
                src_ref=ref.at[edge_of(m)], dst_ref=ref.at[halo_of(opposite(m))],
                send_sem=send.at[m], recv_sem=recv.at[opposite(m)],
                device_id=device, device_id_type=MESH)

        def arrival():
            return pltpu.make_async_remote_copy(
                src_ref=ref.at[edge_of(m)], dst_ref=ref.at[halo_of(m)],
                send_sem=send.at[m], recv_sem=recv.at[m],
                device_id=device, device_id_type=MESH)

        return valid, copy, arrival

    def start(ref, send, recv, messages):
        for m in messages:
            valid, copy, _ = halo(ref, send, recv, m)

            @pl.when(valid)
            def _():
                copy().start()

    def finish(ref, send, recv, messages):
        for m in messages:
            valid, _, arrival = halo(ref, send, recv, m)

            @pl.when(valid)
            def _():
                arrival().wait_recv()

    start(xh, sb, qb, SIDES + UPPER + LOWER)
    loads[1].wait()
    loads[3].wait()
    finish(xh, sb, qb, SIDES)
    inner_taps(xh, w1, acc)
    for row, messages in ((0, UPPER), (1, LOWER)):
        finish(xh, sb, qb, messages)
        hh[1 + row, 1:3] = outer_taps(xh, w1, acc, bb1, row).reshape(2, width, 4 * shard)
        start(hh, sc, qc, SIDES[2 * row : 2 * row + 2] + messages)

    loads[2].wait()
    loads[4].wait()
    finish(hh, sc, qc, SIDES)
    inner_taps(hh, w2, acc)

    def scatter(g, row):
        return pltpu.make_async_remote_copy(
            src_ref=os.at[g, row], dst_ref=ro.at[quarter, row],
            send_sem=se.at[g, row], recv_sem=qe.at[quarter, row],
            device_id={"filt": g}, device_id_type=MESH)

    def scattered(g, row):
        q = quarter_of(g)
        return pltpu.make_async_remote_copy(
            src_ref=os.at[g, row], dst_ref=ro.at[q, row],
            send_sem=se.at[g, row], recv_sem=qe.at[q, row],
            device_id={"filt": g}, device_id_type=MESH)

    for row, messages in ((0, UPPER), (1, LOWER)):
        finish(hh, sc, qc, messages)
        result = outer_taps(hh, w2, acc, bb2, row)
        for g in range(4):
            part = result[:, g * shard : (g + 1) * shard]
            os[g, row] = jnp.concatenate([part[:width], part[width:]], axis=-1)
        for g in peers:
            scatter(g, row).start()
        ro[quarter, row] = os[f, row]

    for g in peers:
        gather(g).wait_send()
    for refs in ((xh, sb, qb), (hh, sc, qc)):
        for m in range(len(MESSAGES)):
            valid, copy, _ = halo(*refs, m)

            @pl.when(valid)
            def _():
                copy().wait_send()

    for row in range(2):
        for g in reversed(peers):
            scattered(g, row).wait_recv()
        for q in range(4):
            for j in range(2):
                out[2 * (q // 2) + row, 2 * (q % 2) + j] = ro[q, row, :, j * shard : (j + 1) * shard]
    for row in range(2):
        for g in peers:
            scatter(g, row).wait_send()


def body(depths, heights, volume, kernel_one, bias_one, kernel_two, bias_two):
    _, _, width, shard = volume.shape
    chans = 4 * shard
    bf16, dma = jnp.bfloat16, pltpu.SemaphoreType.DMA
    packed = pltpu.VMEM((4, 2, width, 2 * shard), bf16)
    padded = pltpu.VMEM((4, 4, width, chans), bf16)
    bias = pltpu.VMEM((1, chans), jnp.float32)
    return pl.pallas_call(
        functools.partial(kernel, depths, heights),
        out_shape=jax.ShapeDtypeStruct(volume.shape, bf16),
        in_specs=[pl.BlockSpec(memory_space=pl.ANY)] * 5,
        out_specs=pl.BlockSpec(memory_space=pltpu.VMEM),
        scratch_shapes=[
            pltpu.VMEM(volume.shape, bf16),
            pltpu.VMEM(kernel_one.shape, bf16),
            pltpu.VMEM(kernel_two.shape, bf16),
            bias,
            bias,
            packed,
            packed,
            padded,
            padded,
            packed,
            packed,
            pltpu.VMEM((3, 2, 2 * width, chans), jnp.float32),
            dma((5,)), dma((4,)), dma((4,)), dma((10,)), dma((10,)), dma((10,)), dma((10,)), dma((4, 2)), dma((4, 2)),
        ],
        compiler_params=pltpu.CompilerParams(
            collective_id=0, has_side_effects=True, vmem_limit_bytes=VMEM_LIMIT),
    )(volume, kernel_one, bias_one.reshape(1, chans), kernel_two, bias_two.reshape(1, chans))


def solution(mesh):
    in_specs = (P("depth", "height", None, "filt"), P(), P(), P(), P())
    out_specs = P("depth", "height", None, "filt")
    step = functools.partial(body, mesh.shape["depth"], mesh.shape["height"])
    return jax.shard_map(step, mesh=mesh, in_specs=in_specs, out_specs=out_specs, check_vma=False)
```

```python
import functools

import jax
import jax.numpy as jnp
from jax import lax
from jax.experimental import pallas as pl
from jax.experimental.pallas import tpu as pltpu
from jax.sharding import PartitionSpec as P

MESH = pl.DeviceIdType.MESH
VMEM_LIMIT = 40_000_000
STEPS = tuple((a, b) for a in (-1, 0, 1) for b in (-1, 0, 1) if (a, b) != (0, 0))
NEAR, FAR, FACE, CORNER, FORWARD = (range(2 * i, 2 * i + 2) for i in range(5))


def flip_of(d):
    return (d % 2) * (1 - (d % 4) // 2)


def leaky(value):
    return jnp.where(value > 0, value, 0.3 * value)


def taps(x, w, rows, count, a, c):
    width, chans = x.shape[2], x.shape[3]
    total = None
    for b in range(3):
        lhs = x[rows : rows + count, b : b + 2].reshape(count * 2 * width, chans)
        part = jnp.dot(lhs, w[a, b, c], preferred_element_type=jnp.float32)
        total = part if total is None else total + part
    return total


def inner_taps(x, w, acc):
    half = 2 * x.shape[2]
    for c in range(3):
        both = taps(x, w, 1, 2, 1, c)
        acc[c, 0] = both[:half] + taps(x, w, 2, 1, 2, c)
        acc[c, 1] = both[half:] + taps(x, w, 1, 1, 0, c)


def outer_taps(x, w, acc, bias, row):
    width, chans = x.shape[2], x.shape[3]
    rows = 2 * width
    low, centre, high = (acc[c, row] + taps(x, w, 3 * row, 1, 2 * row, c) for c in range(3))
    w_of = lax.rem(lax.broadcasted_iota(jnp.int32, (rows, chans), 0), width)
    low = jnp.where(w_of == 0, 0.0, pltpu.roll(low, 1, 0))
    high = jnp.where(w_of == width - 1, 0.0, pltpu.roll(high, rows - 1, 0))
    return leaky(low + centre + high + bias[...]).astype(jnp.bfloat16)


def kernel(
    depths, heights,
    vol, k1, b1, k2, b2, out,
    xv, w1, w2, bb1, bb2, xs, ra, xh, hh, os, ro, acc,
    lsem, sa, qa, sb, qb, sc, qc, se, qe,
):
    d, h, f = lax.axis_index("depth"), lax.axis_index("height"), lax.axis_index("filt")
    flip = flip_of(d)
    width, shard = vol.shape[2], vol.shape[3]

    def quarter_of(g):
        return 2 * ((g // 2 + flip) % 2) + g % 2

    quarter = quarter_of(f)
    peers = [(f + r) % 4 for r in (2, 3, 1)]
    fine_d, fine_h = 2 * d + quarter // 2, 2 * h + f % 2
    def neighbour(sd, sh):
        nd, nh = fine_d + sd, fine_h + sh
        block = nd // 2
        nf = 2 * ((nd + flip_of(block)) % 2) + nh % 2
        valid = (nd >= 0) & (nd < 2 * depths) & (nh >= 0) & (nh < 2 * heights)
        return valid, {"depth": block, "height": nh // 2, "filt": nf}

    loads = [
        pltpu.make_async_copy(src, dst, lsem.at[i])
        for i, (src, dst) in enumerate(((vol, xv), (b1, bb1), (b2, bb2), (k1, w1), (k2, w2)))
    ]
    loads[0].start()
    barrier = pltpu.get_barrier_semaphore()
    for step in STEPS:
        valid, device = neighbour(*step)

        @pl.when(valid)
        def _():
            pl.semaphore_signal(barrier, inc=1, device_id=device, device_id_type=MESH)

    for load in loads[1:]:
        load.start()
    loads[0].wait()
    for q in range(4):
        top, side = 2 * (q // 2), 2 * (q % 2)
        xs[q] = jnp.concatenate([xv[top : top + 2, side], xv[top : top + 2, side + 1]], axis=-1)

    core = f % 2
    outward = 2 * core - 1
    near_edge, near_halo = 2 - core, 3 - 3 * core
    far_edge, far_halo = 1 + core, 3 * core
    has_far = (fine_h + outward >= 0) & (fine_h + outward < 2 * heights)
    has_depth = (fine_d > 0, fine_d < 2 * depths - 1)

    for ref in (xh, hh):
        @pl.when(jnp.logical_not(has_far))
        def _():
            for row in range(4):
                ref[row, far_halo] = jnp.zeros_like(ref[row, far_halo])

        for i in range(2):
            @pl.when(jnp.logical_not(has_depth[i]))
            def _():
                ref[3 * i] = jnp.zeros_like(ref[3 * i])

    tall = 3 - jnp.where(fine_d == 0, 1, 0) - jnp.where(fine_d == 2 * depths - 1, 1, 0)
    wide = 3 - jnp.where(fine_h == 0, 1, 0) - jnp.where(fine_h == 2 * heights - 1, 1, 0)
    pl.semaphore_wait(barrier, tall * wide - 1)

    def gather(g):
        return pltpu.make_async_remote_copy(
            src_ref=xs.at[quarter_of(g)], dst_ref=ra.at[f], send_sem=sa.at[g], recv_sem=qa.at[f],
            device_id={"filt": g}, device_id_type=MESH)

    def gathered(g):
        return pltpu.make_async_remote_copy(
            src_ref=xs.at[quarter], dst_ref=ra.at[g], send_sem=sa.at[g], recv_sem=qa.at[g],
            device_id={"filt": g}, device_id_type=MESH)

    for g in peers:
        gather(g).start()
    ra[f] = xs[quarter]
    for g in reversed(peers):
        gathered(g).wait_recv()
    for i in range(2):
        for j in range(2):
            xh[1 + i, 1 + j] = jnp.concatenate(
                [ra[g, i, :, j * shard : (j + 1) * shard] for g in range(4)], axis=-1)

    def halo(ref, send, recv, m):
        i, whole = m % 2, pl.ds(1, 2)
        if m in NEAR:
            valid, to, step = None, m, (0, -outward)
            edge, there, here = (1 + i, near_edge), (1 + i, 3 * core), (1 + i, near_halo)
        elif m in FAR:
            valid, to, step = has_far, m, (0, outward)
            edge, there, here = (1 + i, far_edge), (1 + i, 3 - 3 * core), (1 + i, far_halo)
        elif m in FACE:
            valid, to, step = has_depth[i], FACE[1 - i], (2 * i - 1, 0)
            edge, there, here = (1 + i, whole), (3 - 3 * i, whole), (3 * i, whole)
        elif m in CORNER:
            valid, to, step = has_depth[i] & has_far, CORNER[1 - i], (2 * i - 1, outward)
            edge, there, here = (1 + i, far_edge), (3 - 3 * i, 3 - 3 * core), (3 * i, far_halo)
        else:
            valid, to, step = has_depth[i], m, (0, -outward)
            edge, there, here = (3 * i, near_edge), (3 * i, 3 * core), (3 * i, near_halo)
        _, device = neighbour(*step)

        def copy():
            return pltpu.make_async_remote_copy(
                src_ref=ref.at[edge], dst_ref=ref.at[there],
                send_sem=send.at[m], recv_sem=recv.at[to],
                device_id=device, device_id_type=MESH)

        def arrival():
            return pltpu.make_async_remote_copy(
                src_ref=ref.at[edge], dst_ref=ref.at[here],
                send_sem=send.at[m], recv_sem=recv.at[m],
                device_id=device, device_id_type=MESH)

        return valid, copy, arrival

    def when(valid, act):
        if valid is None:
            act()
        else:
            pl.when(valid)(act)

    def start(refs, *messages):
        for m in messages:
            valid, copy, _ = halo(*refs, m)
            when(valid, lambda: copy().start())

    def finish(refs, *messages):
        for m in messages:
            valid, _, arrival = halo(*refs, m)
            when(valid, lambda: arrival().wait_recv())

    def forward(refs, i):
        valid, _, arrival = halo(*refs, FACE[i])
        _, copy, _ = halo(*refs, FORWARD[i])

        @pl.when(valid)
        def _():
            arrival().wait_recv()
            copy().start()

    first, second = (xh, sb, qb), (hh, sc, qc)
    start(first, *FACE, *FAR, *CORNER, *NEAR)
    loads[1].wait()
    loads[3].wait()
    finish(first, *NEAR, *FAR)
    inner_taps(xh, w1, acc)
    forward(first, 0)
    forward(first, 1)
    for row in range(2):
        finish(first, CORNER[row], FORWARD[row])
        hh[1 + row, 1:3] = outer_taps(xh, w1, acc, bb1, row).reshape(2, width, 4 * shard)
        start(second, FACE[row], FAR[row], CORNER[row], NEAR[row])

    loads[2].wait()
    loads[4].wait()
    finish(second, *NEAR, *FAR)
    inner_taps(hh, w2, acc)
    forward(second, 0)
    forward(second, 1)

    def scatter(g, row):
        return pltpu.make_async_remote_copy(
            src_ref=os.at[g, row], dst_ref=ro.at[quarter, row],
            send_sem=se.at[g, row], recv_sem=qe.at[quarter, row],
            device_id={"filt": g}, device_id_type=MESH)

    def scattered(g, row):
        q = quarter_of(g)
        return pltpu.make_async_remote_copy(
            src_ref=os.at[g, row], dst_ref=ro.at[q, row],
            send_sem=se.at[g, row], recv_sem=qe.at[q, row],
            device_id={"filt": g}, device_id_type=MESH)

    for row in range(2):
        finish(second, CORNER[row], FORWARD[row])
        result = outer_taps(hh, w2, acc, bb2, row)
        for g in range(4):
            part = result[:, g * shard : (g + 1) * shard]
            os[g, row] = jnp.concatenate([part[:width], part[width:]], axis=-1)
        for g in peers:
            scatter(g, row).start()
        ro[quarter, row] = os[f, row]

    for g in peers:
        gather(g).wait_send()
    for refs in (first, second):
        for m in range(10):
            valid, copy, _ = halo(*refs, m)
            when(valid, lambda: copy().wait_send())

    for row in range(2):
        for g in reversed(peers):
            scattered(g, row).wait_recv()
        for q in range(4):
            for j in range(2):
                out[2 * (q // 2) + row, 2 * (q % 2) + j] = ro[q, row, :, j * shard : (j + 1) * shard]
    for row in range(2):
        for g in peers:
            scatter(g, row).wait_send()


def body(depths, heights, volume, kernel_one, bias_one, kernel_two, bias_two):
    _, _, width, shard = volume.shape
    chans = 4 * shard
    bf16, dma = jnp.bfloat16, pltpu.SemaphoreType.DMA
    packed = pltpu.VMEM((4, 2, width, 2 * shard), bf16)
    padded = pltpu.VMEM((4, 4, width, chans), bf16)
    bias = pltpu.VMEM((1, chans), jnp.float32)
    return pl.pallas_call(
        functools.partial(kernel, depths, heights),
        out_shape=jax.ShapeDtypeStruct(volume.shape, bf16),
        in_specs=[pl.BlockSpec(memory_space=pltpu.HBM)] * 5,
        out_specs=pl.BlockSpec(memory_space=pltpu.VMEM),
        scratch_shapes=[
            pltpu.VMEM(volume.shape, bf16),
            pltpu.VMEM(kernel_one.shape, bf16),
            pltpu.VMEM(kernel_two.shape, bf16),
            bias,
            bias,
            packed,
            packed,
            padded,
            padded,
            packed,
            packed,
            pltpu.VMEM((3, 2, 2 * width, chans), jnp.float32),
            dma((5,)), dma((4,)), dma((4,)), dma((10,)), dma((10,)), dma((10,)), dma((10,)), dma((4, 2)), dma((4, 2)),
        ],
        compiler_params=pltpu.CompilerParams(
            collective_id=0, has_side_effects=True, vmem_limit_bytes=VMEM_LIMIT),
    )(*(pltpu.with_memory_space_constraint(v, pltpu.HBM) for v in (volume, kernel_one, bias_one.reshape(1, chans), kernel_two, bias_two.reshape(1, chans))))


def solution(mesh):
    in_specs = (P("depth", "height", None, "filt"), P(), P(), P(), P())
    out_specs = P("depth", "height", None, "filt")
    step = functools.partial(body, mesh.shape["depth"], mesh.shape["height"])
    return jax.shard_map(step, mesh=mesh, in_specs=in_specs, out_specs=out_specs, check_vma=False)
```

```python
import functools

import jax
import jax.numpy as jnp
from jax import lax
from jax.experimental import pallas as pl
from jax.experimental.pallas import tpu as pltpu
from jax.sharding import PartitionSpec as P

MESH = pl.DeviceIdType.MESH
VMEM_LIMIT = 40_000_000
STEPS = tuple((a, b) for a in (-1, 0, 1) for b in (-1, 0, 1) if (a, b) != (0, 0))
NEAR, FAR, FACE, REST, CORNER, FORWARD = (range(2 * i, 2 * i + 2) for i in range(6))


def flip_of(d):
    return (d % 2) * (1 - (d % 4) // 2)


def leaky(value):
    return jnp.where(value > 0, value, 0.3 * value)


def taps(x, w, rows, count, a, c):
    width, chans = x.shape[2], x.shape[3]
    total = None
    for b in range(3):
        lhs = x[rows : rows + count, b : b + 2].reshape(count * 2 * width, chans)
        part = jnp.dot(lhs, w[a, b, c], preferred_element_type=jnp.float32)
        total = part if total is None else total + part
    return total


def inner_taps(x, w, acc):
    half = 2 * x.shape[2]
    for c in range(3):
        both = taps(x, w, 1, 2, 1, c)
        acc[c, 0] = both[:half] + taps(x, w, 2, 1, 2, c)
        acc[c, 1] = both[half:] + taps(x, w, 1, 1, 0, c)


def outer_taps(x, w, acc, bias, row):
    width, chans = x.shape[2], x.shape[3]
    rows = 2 * width
    low, centre, high = (acc[c, row] + taps(x, w, 3 * row, 1, 2 * row, c) for c in range(3))
    w_of = lax.rem(lax.broadcasted_iota(jnp.int32, (rows, chans), 0), width)
    low = jnp.where(w_of == 0, 0.0, pltpu.roll(low, 1, 0))
    high = jnp.where(w_of == width - 1, 0.0, pltpu.roll(high, rows - 1, 0))
    return leaky(low + centre + high + bias[...]).astype(jnp.bfloat16)


def kernel(
    depths, heights,
    vol, k1, b1, k2, b2, out,
    xv, w1, w2, bb1, bb2, xs, ra, xh, hh, os, ro, acc,
    lsem, sa, qa, sb, qb, sc, qc, se, qe,
):
    d, h, f = lax.axis_index("depth"), lax.axis_index("height"), lax.axis_index("filt")
    flip = flip_of(d)
    width, shard = vol.shape[2], vol.shape[3]

    def quarter_of(g):
        return 2 * ((g // 2 + flip) % 2) + g % 2

    quarter = quarter_of(f)
    peers = [(f + r) % 4 for r in (2, 3, 1)]
    fine_d, fine_h = 2 * d + quarter // 2, 2 * h + f % 2
    def neighbour(sd, sh):
        nd, nh = fine_d + sd, fine_h + sh
        block = nd // 2
        nf = 2 * ((nd + flip_of(block)) % 2) + nh % 2
        valid = (nd >= 0) & (nd < 2 * depths) & (nh >= 0) & (nh < 2 * heights)
        return valid, {"depth": block, "height": nh // 2, "filt": nf}

    loads = [
        pltpu.make_async_copy(src, dst, lsem.at[i])
        for i, (src, dst) in enumerate(((vol, xv), (b1, bb1), (b2, bb2), (k1, w1), (k2, w2)))
    ]
    loads[0].start()
    barrier = pltpu.get_barrier_semaphore()
    for step in STEPS:
        valid, device = neighbour(*step)

        @pl.when(valid)
        def _():
            pl.semaphore_signal(barrier, inc=1, device_id=device, device_id_type=MESH)

    for load in loads[1:]:
        load.start()
    loads[0].wait()
    for q in range(4):
        top, side = 2 * (q // 2), 2 * (q % 2)
        xs[q] = jnp.concatenate([xv[top : top + 2, side], xv[top : top + 2, side + 1]], axis=-1)

    core = f % 2
    outward = 2 * core - 1
    near_edge, near_halo = 2 - core, 3 - 3 * core
    far_edge, far_halo = 1 + core, 3 * core
    has_far = (fine_h + outward >= 0) & (fine_h + outward < 2 * heights)
    has_depth = (fine_d > 0, fine_d < 2 * depths - 1)

    for ref in (xh, hh):
        @pl.when(jnp.logical_not(has_far))
        def _():
            for row in range(4):
                ref[row, far_halo] = jnp.zeros_like(ref[row, far_halo])

        for i in range(2):
            @pl.when(jnp.logical_not(has_depth[i]))
            def _():
                ref[3 * i] = jnp.zeros_like(ref[3 * i])

    tall = 3 - jnp.where(fine_d == 0, 1, 0) - jnp.where(fine_d == 2 * depths - 1, 1, 0)
    wide = 3 - jnp.where(fine_h == 0, 1, 0) - jnp.where(fine_h == 2 * heights - 1, 1, 0)
    pl.semaphore_wait(barrier, tall * wide - 1)

    def gather(g):
        return pltpu.make_async_remote_copy(
            src_ref=xs.at[quarter_of(g)], dst_ref=ra.at[f], send_sem=sa.at[g], recv_sem=qa.at[f],
            device_id={"filt": g}, device_id_type=MESH)

    def gathered(g):
        return pltpu.make_async_remote_copy(
            src_ref=xs.at[quarter], dst_ref=ra.at[g], send_sem=sa.at[g], recv_sem=qa.at[g],
            device_id={"filt": g}, device_id_type=MESH)

    for g in peers:
        gather(g).start()
    ra[f] = xs[quarter]
    for g in reversed(peers):
        gathered(g).wait_recv()
    for i in range(2):
        for j in range(2):
            xh[1 + i, 1 + j] = jnp.concatenate(
                [ra[g, i, :, j * shard : (j + 1) * shard] for g in range(4)], axis=-1)

    def halo(ref, send, recv, m):
        i = m % 2
        if m in NEAR:
            valid, to, step = None, m, (0, -outward)
            edge, there, here = (1 + i, near_edge), (1 + i, 3 * core), (1 + i, near_halo)
        elif m in FAR:
            valid, to, step = has_far, m, (0, outward)
            edge, there, here = (1 + i, far_edge), (1 + i, 3 - 3 * core), (1 + i, far_halo)
        elif m in FACE:
            valid, to, step = has_depth[i], FACE[1 - i], (2 * i - 1, 0)
            edge, there, here = (1 + i, near_edge), (3 - 3 * i, near_edge), (3 * i, near_edge)
        elif m in REST:
            valid, to, step = has_depth[i], REST[1 - i], (2 * i - 1, 0)
            edge, there, here = (1 + i, far_edge), (3 - 3 * i, far_edge), (3 * i, far_edge)
        elif m in CORNER:
            valid, to, step = has_depth[i] & has_far, CORNER[1 - i], (2 * i - 1, outward)
            edge, there, here = (1 + i, far_edge), (3 - 3 * i, 3 - 3 * core), (3 * i, far_halo)
        else:
            valid, to, step = has_depth[i], m, (0, -outward)
            edge, there, here = (3 * i, near_edge), (3 * i, 3 * core), (3 * i, near_halo)
        _, device = neighbour(*step)

        def copy():
            return pltpu.make_async_remote_copy(
                src_ref=ref.at[edge], dst_ref=ref.at[there],
                send_sem=send.at[m], recv_sem=recv.at[to],
                device_id=device, device_id_type=MESH)

        def arrival():
            return pltpu.make_async_remote_copy(
                src_ref=ref.at[edge], dst_ref=ref.at[here],
                send_sem=send.at[m], recv_sem=recv.at[m],
                device_id=device, device_id_type=MESH)

        return valid, copy, arrival

    def when(valid, act):
        if valid is None:
            act()
        else:
            pl.when(valid)(act)

    def start(refs, *messages):
        for m in messages:
            valid, copy, _ = halo(*refs, m)
            when(valid, lambda: copy().start())

    def finish(refs, *messages):
        for m in messages:
            valid, _, arrival = halo(*refs, m)
            when(valid, lambda: arrival().wait_recv())

    def forward(refs, i):
        valid, _, arrival = halo(*refs, FACE[i])
        _, copy, _ = halo(*refs, FORWARD[i])

        @pl.when(valid)
        def _():
            arrival().wait_recv()
            copy().start()

    first, second = (xh, sb, qb), (hh, sc, qc)
    start(first, *FACE, *FAR, *CORNER, *REST, *NEAR)
    loads[1].wait()
    loads[3].wait()
    forward(first, 0)
    forward(first, 1)
    finish(first, *NEAR, *FAR)
    inner_taps(xh, w1, acc)
    for row in range(2):
        finish(first, FORWARD[row], CORNER[row], REST[row])
        hh[1 + row, 1:3] = outer_taps(xh, w1, acc, bb1, row).reshape(2, width, 4 * shard)
        start(second, FACE[row], FAR[row], CORNER[row], REST[row], NEAR[row])

    loads[2].wait()
    loads[4].wait()
    forward(second, 0)
    forward(second, 1)
    finish(second, *NEAR, *FAR)
    inner_taps(hh, w2, acc)

    def scatter(g, row):
        return pltpu.make_async_remote_copy(
            src_ref=os.at[g, row], dst_ref=ro.at[quarter, row],
            send_sem=se.at[g, row], recv_sem=qe.at[quarter, row],
            device_id={"filt": g}, device_id_type=MESH)

    def scattered(g, row):
        q = quarter_of(g)
        return pltpu.make_async_remote_copy(
            src_ref=os.at[g, row], dst_ref=ro.at[q, row],
            send_sem=se.at[g, row], recv_sem=qe.at[q, row],
            device_id={"filt": g}, device_id_type=MESH)

    for row in range(2):
        finish(second, FORWARD[row], CORNER[row], REST[row])
        result = outer_taps(hh, w2, acc, bb2, row)
        for g in range(4):
            part = result[:, g * shard : (g + 1) * shard]
            os[g, row] = jnp.concatenate([part[:width], part[width:]], axis=-1)
        for g in peers:
            scatter(g, row).start()
        ro[quarter, row] = os[f, row]

    for g in peers:
        gather(g).wait_send()
    for refs in (first, second):
        for m in range(12):
            valid, copy, _ = halo(*refs, m)
            when(valid, lambda: copy().wait_send())

    for row in range(2):
        for g in reversed(peers):
            scattered(g, row).wait_recv()
        for q in range(4):
            for j in range(2):
                out[2 * (q // 2) + row, 2 * (q % 2) + j] = ro[q, row, :, j * shard : (j + 1) * shard]
    for row in range(2):
        for g in peers:
            scatter(g, row).wait_send()


def body(depths, heights, volume, kernel_one, bias_one, kernel_two, bias_two):
    _, _, width, shard = volume.shape
    chans = 4 * shard
    bf16, dma = jnp.bfloat16, pltpu.SemaphoreType.DMA
    packed = pltpu.VMEM((4, 2, width, 2 * shard), bf16)
    padded = pltpu.VMEM((4, 4, width, chans), bf16)
    bias = pltpu.VMEM((1, chans), jnp.float32)
    return pl.pallas_call(
        functools.partial(kernel, depths, heights),
        out_shape=jax.ShapeDtypeStruct(volume.shape, bf16),
        in_specs=[pl.BlockSpec(memory_space=pltpu.HBM)] * 5,
        out_specs=pl.BlockSpec(memory_space=pltpu.VMEM),
        scratch_shapes=[
            pltpu.VMEM(volume.shape, bf16),
            pltpu.VMEM(kernel_one.shape, bf16),
            pltpu.VMEM(kernel_two.shape, bf16),
            bias,
            bias,
            packed,
            packed,
            padded,
            padded,
            packed,
            packed,
            pltpu.VMEM((3, 2, 2 * width, chans), jnp.float32),
            dma((5,)), dma((4,)), dma((4,)), dma((12,)), dma((12,)), dma((12,)), dma((12,)), dma((4, 2)), dma((4, 2)),
        ],
        compiler_params=pltpu.CompilerParams(
            collective_id=0, has_side_effects=True, vmem_limit_bytes=VMEM_LIMIT),
    )(*(pltpu.with_memory_space_constraint(v, pltpu.HBM) for v in (volume, kernel_one, bias_one.reshape(1, chans), kernel_two, bias_two.reshape(1, chans))))


def solution(mesh):
    in_specs = (P("depth", "height", None, "filt"), P(), P(), P(), P())
    out_specs = P("depth", "height", None, "filt")
    step = functools.partial(body, mesh.shape["depth"], mesh.shape["height"])
    return jax.shard_map(step, mesh=mesh, in_specs=in_specs, out_specs=out_specs, check_vma=False)
```

```python
import functools

import jax
import jax.numpy as jnp
from jax import lax
from jax.experimental import pallas as pl
from jax.experimental.pallas import tpu as pltpu
from jax.sharding import PartitionSpec as P

MESH = pl.DeviceIdType.MESH
VMEM_LIMIT = 40_000_000
STEPS = tuple((a, b) for a in (-1, 0, 1) for b in (-1, 0, 1) if (a, b) != (0, 0))
NEAR, FAR, FACE, REST, CORNER, FORWARD = (range(2 * i, 2 * i + 2) for i in range(6))


def flip_of(d):
    return (d % 2) * (1 - (d % 4) // 2)


def leaky(value):
    return jnp.where(value > 0, value, 0.3 * value)


def taps(x, w, rows, count, a, c):
    width, chans = x.shape[2], x.shape[3]
    total = None
    for b in range(3):
        lhs = x[rows : rows + count, b : b + 2].reshape(count * 2 * width, chans)
        part = jnp.dot(lhs, w[a, b, c], preferred_element_type=jnp.float32)
        total = part if total is None else total + part
    return total


def inner_taps(x, w, acc):
    half = 2 * x.shape[2]
    for c in range(3):
        both = taps(x, w, 1, 2, 1, c)
        acc[c, 0] = both[:half] + taps(x, w, 2, 1, 2, c)
        acc[c, 1] = both[half:] + taps(x, w, 1, 1, 0, c)


def outer_taps(x, w, acc, bias, row):
    width, chans = x.shape[2], x.shape[3]
    rows = 2 * width
    low, centre, high = (acc[c, row] + taps(x, w, 3 * row, 1, 2 * row, c) for c in range(3))
    w_of = lax.rem(lax.broadcasted_iota(jnp.int32, (rows, chans), 0), width)
    low = jnp.where(w_of == 0, 0.0, pltpu.roll(low, 1, 0))
    high = jnp.where(w_of == width - 1, 0.0, pltpu.roll(high, rows - 1, 0))
    return leaky(low + centre + high + bias[...]).astype(jnp.bfloat16)


def kernel(
    depths, heights,
    vol, k1, b1, k2, b2, out,
    xv, w1, w2, bb1, bb2, xs, ra, xh, hh, os, ro, acc,
    lsem, sa, qa, sb, qb, sc, qc, se, qe,
):
    d, h, f = lax.axis_index("depth"), lax.axis_index("height"), lax.axis_index("filt")
    flip = flip_of(d)
    width, shard = vol.shape[2], vol.shape[3]

    def quarter_of(g):
        return 2 * ((g // 2 + flip) % 2) + g % 2

    quarter = quarter_of(f)
    peers = [(f + r) % 4 for r in (2, 3, 1)]
    fine_d, fine_h = 2 * d + quarter // 2, 2 * h + f % 2
    def neighbour(sd, sh):
        nd, nh = fine_d + sd, fine_h + sh
        block = nd // 2
        nf = 2 * ((nd + flip_of(block)) % 2) + nh % 2
        valid = (nd >= 0) & (nd < 2 * depths) & (nh >= 0) & (nh < 2 * heights)
        return valid, {"depth": block, "height": nh // 2, "filt": nf}

    loads = [
        pltpu.make_async_copy(src, dst, lsem.at[i])
        for i, (src, dst) in enumerate(((vol, xv), (b1, bb1), (b2, bb2), (k1, w1), (k2, w2)))
    ]
    loads[0].start()
    barrier = pltpu.get_barrier_semaphore()
    for step in STEPS:
        valid, device = neighbour(*step)

        @pl.when(valid)
        def _():
            pl.semaphore_signal(barrier, inc=1, device_id=device, device_id_type=MESH)

    loads[0].wait()
    for q in range(4):
        top, side = 2 * (q // 2), 2 * (q % 2)
        xs[q] = jnp.concatenate([xv[top : top + 2, side], xv[top : top + 2, side + 1]], axis=-1)

    core = f % 2
    outward = 2 * core - 1
    near_edge, near_halo = 2 - core, 3 - 3 * core
    far_edge, far_halo = 1 + core, 3 * core
    has_far = (fine_h + outward >= 0) & (fine_h + outward < 2 * heights)
    has_depth = (fine_d > 0, fine_d < 2 * depths - 1)

    for ref in (xh, hh):
        @pl.when(jnp.logical_not(has_far))
        def _():
            for row in range(4):
                ref[row, far_halo] = jnp.zeros_like(ref[row, far_halo])

        for i in range(2):
            @pl.when(jnp.logical_not(has_depth[i]))
            def _():
                ref[3 * i] = jnp.zeros_like(ref[3 * i])

    tall = 3 - jnp.where(fine_d == 0, 1, 0) - jnp.where(fine_d == 2 * depths - 1, 1, 0)
    wide = 3 - jnp.where(fine_h == 0, 1, 0) - jnp.where(fine_h == 2 * heights - 1, 1, 0)
    pl.semaphore_wait(barrier, tall * wide - 1)

    def gather(g):
        return pltpu.make_async_remote_copy(
            src_ref=xs.at[quarter_of(g)], dst_ref=ra.at[f], send_sem=sa.at[g], recv_sem=qa.at[f],
            device_id={"filt": g}, device_id_type=MESH)

    def gathered(g):
        return pltpu.make_async_remote_copy(
            src_ref=xs.at[quarter], dst_ref=ra.at[g], send_sem=sa.at[g], recv_sem=qa.at[g],
            device_id={"filt": g}, device_id_type=MESH)

    for g in peers:
        gather(g).start()
    for load in loads[1:4]:
        load.start()
    ra[f] = xs[quarter]
    for g in reversed(peers):
        gathered(g).wait_recv()
    for i in range(2):
        for j in range(2):
            xh[1 + i, 1 + j] = jnp.concatenate(
                [ra[g, i, :, j * shard : (j + 1) * shard] for g in range(4)], axis=-1)

    def halo(ref, send, recv, m):
        i = m % 2
        if m in NEAR:
            valid, to, step = None, m, (0, -outward)
            edge, there, here = (1 + i, near_edge), (1 + i, 3 * core), (1 + i, near_halo)
        elif m in FAR:
            valid, to, step = has_far, m, (0, outward)
            edge, there, here = (1 + i, far_edge), (1 + i, 3 - 3 * core), (1 + i, far_halo)
        elif m in FACE:
            valid, to, step = has_depth[i], FACE[1 - i], (2 * i - 1, 0)
            edge, there, here = (1 + i, near_edge), (3 - 3 * i, near_edge), (3 * i, near_edge)
        elif m in REST:
            valid, to, step = has_depth[i], REST[1 - i], (2 * i - 1, 0)
            edge, there, here = (1 + i, far_edge), (3 - 3 * i, far_edge), (3 * i, far_edge)
        elif m in CORNER:
            valid, to, step = has_depth[i] & has_far, CORNER[1 - i], (2 * i - 1, outward)
            edge, there, here = (1 + i, far_edge), (3 - 3 * i, 3 - 3 * core), (3 * i, far_halo)
        else:
            valid, to, step = has_depth[i], m, (0, -outward)
            edge, there, here = (3 * i, near_edge), (3 * i, 3 * core), (3 * i, near_halo)
        _, device = neighbour(*step)

        def copy():
            return pltpu.make_async_remote_copy(
                src_ref=ref.at[edge], dst_ref=ref.at[there],
                send_sem=send.at[m], recv_sem=recv.at[to],
                device_id=device, device_id_type=MESH)

        def arrival():
            return pltpu.make_async_remote_copy(
                src_ref=ref.at[edge], dst_ref=ref.at[here],
                send_sem=send.at[m], recv_sem=recv.at[m],
                device_id=device, device_id_type=MESH)

        return valid, copy, arrival

    def when(valid, act):
        if valid is None:
            act()
        else:
            pl.when(valid)(act)

    def start(refs, *messages):
        for m in messages:
            valid, copy, _ = halo(*refs, m)
            when(valid, lambda: copy().start())

    def finish(refs, *messages):
        for m in messages:
            valid, _, arrival = halo(*refs, m)
            when(valid, lambda: arrival().wait_recv())

    def forward(refs, i):
        valid, _, arrival = halo(*refs, FACE[i])
        _, copy, _ = halo(*refs, FORWARD[i])

        @pl.when(valid)
        def _():
            arrival().wait_recv()
            copy().start()

    first, second = (xh, sb, qb), (hh, sc, qc)
    start(first, *FACE, *FAR, *CORNER, *REST, *NEAR)
    loads[4].start()
    loads[1].wait()
    loads[3].wait()
    forward(first, 0)
    forward(first, 1)
    finish(first, *NEAR, *FAR)
    inner_taps(xh, w1, acc)
    for row in range(2):
        finish(first, FORWARD[row], CORNER[row], REST[row])
        hh[1 + row, 1:3] = outer_taps(xh, w1, acc, bb1, row).reshape(2, width, 4 * shard)
        start(second, FACE[row], FAR[row], CORNER[row], REST[row], NEAR[row])

    loads[2].wait()
    loads[4].wait()
    forward(second, 0)
    forward(second, 1)
    finish(second, *NEAR, *FAR)
    inner_taps(hh, w2, acc)

    def scatter(g, row):
        return pltpu.make_async_remote_copy(
            src_ref=os.at[g, row], dst_ref=ro.at[quarter, row],
            send_sem=se.at[g, row], recv_sem=qe.at[quarter, row],
            device_id={"filt": g}, device_id_type=MESH)

    def scattered(g, row):
        q = quarter_of(g)
        return pltpu.make_async_remote_copy(
            src_ref=os.at[g, row], dst_ref=ro.at[q, row],
            send_sem=se.at[g, row], recv_sem=qe.at[q, row],
            device_id={"filt": g}, device_id_type=MESH)

    for row in range(2):
        finish(second, FORWARD[row], CORNER[row], REST[row])
        result = outer_taps(hh, w2, acc, bb2, row)
        for g in range(4):
            part = result[:, g * shard : (g + 1) * shard]
            os[g, row] = jnp.concatenate([part[:width], part[width:]], axis=-1)
        for g in peers:
            scatter(g, row).start()
        ro[quarter, row] = os[f, row]

    for g in peers:
        gather(g).wait_send()
    for refs in (first, second):
        for m in range(12):
            valid, copy, _ = halo(*refs, m)
            when(valid, lambda: copy().wait_send())

    for row in range(2):
        for g in reversed(peers):
            scattered(g, row).wait_recv()
        for q in range(4):
            for j in range(2):
                out[2 * (q // 2) + row, 2 * (q % 2) + j] = ro[q, row, :, j * shard : (j + 1) * shard]
    for row in range(2):
        for g in peers:
            scatter(g, row).wait_send()


def body(depths, heights, volume, kernel_one, bias_one, kernel_two, bias_two):
    _, _, width, shard = volume.shape
    chans = 4 * shard
    bf16, dma = jnp.bfloat16, pltpu.SemaphoreType.DMA
    packed = pltpu.VMEM((4, 2, width, 2 * shard), bf16)
    padded = pltpu.VMEM((4, 4, width, chans), bf16)
    bias = pltpu.VMEM((1, chans), jnp.float32)
    return pl.pallas_call(
        functools.partial(kernel, depths, heights),
        out_shape=jax.ShapeDtypeStruct(volume.shape, bf16),
        in_specs=[pl.BlockSpec(memory_space=pltpu.HBM)] * 5,
        out_specs=pl.BlockSpec(memory_space=pltpu.VMEM),
        scratch_shapes=[
            pltpu.VMEM(volume.shape, bf16),
            pltpu.VMEM(kernel_one.shape, bf16),
            pltpu.VMEM(kernel_two.shape, bf16),
            bias,
            bias,
            packed,
            packed,
            padded,
            padded,
            packed,
            packed,
            pltpu.VMEM((3, 2, 2 * width, chans), jnp.float32),
            dma((5,)), dma((4,)), dma((4,)), dma((12,)), dma((12,)), dma((12,)), dma((12,)), dma((4, 2)), dma((4, 2)),
        ],
        compiler_params=pltpu.CompilerParams(
            collective_id=0, has_side_effects=True, vmem_limit_bytes=VMEM_LIMIT),
    )(*(pltpu.with_memory_space_constraint(v, pltpu.HBM) for v in (volume, kernel_one, bias_one.reshape(1, chans), kernel_two, bias_two.reshape(1, chans))))


def solution(mesh):
    in_specs = (P("depth", "height", None, "filt"), P(), P(), P(), P())
    out_specs = P("depth", "height", None, "filt")
    step = functools.partial(body, mesh.shape["depth"], mesh.shape["height"])
    return jax.shard_map(step, mesh=mesh, in_specs=in_specs, out_specs=out_specs, check_vma=False)
```

```python
import functools

import jax
import jax.numpy as jnp
from jax import lax
from jax.experimental import pallas as pl
from jax.experimental.pallas import tpu as pltpu
from jax.sharding import PartitionSpec as P

MESH = pl.DeviceIdType.MESH
VMEM_LIMIT = 40_000_000
STEPS = tuple((a, b) for a in (-1, 0, 1) for b in (-1, 0, 1) if (a, b) != (0, 0))
NEAR, FAR, FACE, REST, CORNER, FORWARD = range(6)


def flip_of(d):
    return (d % 2) * (1 - (d % 4) // 2)


def leaky(value):
    return jnp.where(value > 0, value, 0.3 * value)


def taps(x, w, rows, count, a, c):
    width, chans = x.shape[2], x.shape[3]
    total = None
    for b in range(3):
        lhs = x[pl.ds(rows, count), b : b + 2].reshape(count * 2 * width, chans)
        part = jnp.dot(lhs, w[a, b, c], preferred_element_type=jnp.float32)
        total = part if total is None else total + part
    return total


def inner_taps(x, w, acc):
    half = 2 * x.shape[2]
    for c in range(3):
        both = taps(x, w, 1, 2, 1, c)
        acc[c, 0] = both[:half] + taps(x, w, 2, 1, 2, c)
        acc[c, 1] = both[half:] + taps(x, w, 1, 1, 0, c)


def outer_taps(x, w, acc, bias, row):
    width, chans = x.shape[2], x.shape[3]
    rows = 2 * width
    low, centre, high = (acc[c, row] + taps(x, w, 3 * row, 1, 2 * row, c) for c in range(3))
    w_of = lax.rem(lax.broadcasted_iota(jnp.int32, (rows, chans), 0), width)
    low = jnp.where(w_of == 0, 0.0, pltpu.roll(low, 1, 0))
    high = jnp.where(w_of == width - 1, 0.0, pltpu.roll(high, rows - 1, 0))
    return leaky(low + centre + high + bias[...]).astype(jnp.bfloat16)


def kernel(
    depths, heights,
    vol, k1, b1, k2, b2, out,
    xv, w1, w2, bb1, bb2, xs, ra, xh, hh, os, ro, acc,
    lsem, sa, qa, sb, qb, sc, qc, se, qe,
):
    d, h, f = lax.axis_index("depth"), lax.axis_index("height"), lax.axis_index("filt")
    flip = flip_of(d)
    width, shard = vol.shape[2], vol.shape[3]

    def quarter_of(g):
        return 2 * ((g // 2 + flip) % 2) + g % 2

    quarter = quarter_of(f)
    peers = [(f + r) % 4 for r in (2, 3, 1)]
    order = (1 - quarter // 2, quarter // 2)
    fine_d, fine_h = 2 * d + quarter // 2, 2 * h + f % 2
    def neighbour(sd, sh):
        nd, nh = fine_d + sd, fine_h + sh
        block = nd // 2
        nf = 2 * ((nd + flip_of(block)) % 2) + nh % 2
        valid = (nd >= 0) & (nd < 2 * depths) & (nh >= 0) & (nh < 2 * heights)
        return valid, {"depth": block, "height": nh // 2, "filt": nf}

    loads = [
        pltpu.make_async_copy(src, dst, lsem.at[i])
        for i, (src, dst) in enumerate(((vol, xv), (b1, bb1), (b2, bb2), (k1, w1), (k2, w2)))
    ]
    loads[0].start()
    barrier = pltpu.get_barrier_semaphore()
    for step in STEPS:
        valid, device = neighbour(*step)

        @pl.when(valid)
        def _():
            pl.semaphore_signal(barrier, inc=1, device_id=device, device_id_type=MESH)

    for load in loads[1:]:
        load.start()
    loads[0].wait()
    for q in range(4):
        top, side = 2 * (q // 2), 2 * (q % 2)
        xs[q] = jnp.concatenate([xv[top : top + 2, side], xv[top : top + 2, side + 1]], axis=-1)

    core = f % 2
    outward = 2 * core - 1
    near_edge, near_halo = 2 - core, 3 - 3 * core
    far_edge, far_halo = 1 + core, 3 * core
    has_far = (fine_h + outward >= 0) & (fine_h + outward < 2 * heights)

    def has_depth(i):
        nd = fine_d + 2 * i - 1
        return (nd >= 0) & (nd < 2 * depths)

    for ref in (xh, hh):
        @pl.when(jnp.logical_not(has_far))
        def _():
            for row in range(4):
                ref[row, far_halo] = jnp.zeros_like(ref[row, far_halo])

        for i in range(2):
            @pl.when(jnp.logical_not(has_depth(i)))
            def _():
                ref[3 * i] = jnp.zeros_like(ref[3 * i])

    tall = 3 - jnp.where(fine_d == 0, 1, 0) - jnp.where(fine_d == 2 * depths - 1, 1, 0)
    wide = 3 - jnp.where(fine_h == 0, 1, 0) - jnp.where(fine_h == 2 * heights - 1, 1, 0)
    pl.semaphore_wait(barrier, tall * wide - 1)

    def gather(g, p):
        q = quarter_of(g)
        row = q // 2 if p else 1 - q // 2
        return pltpu.make_async_remote_copy(
            src_ref=xs.at[q, row], dst_ref=ra.at[f, row], send_sem=sa.at[g, p], recv_sem=qa.at[f, p],
            device_id={"filt": g}, device_id_type=MESH)

    def gathered(g, p):
        return pltpu.make_async_remote_copy(
            src_ref=xs.at[quarter, order[p]], dst_ref=ra.at[g, order[p]], send_sem=sa.at[g, p], recv_sem=qa.at[g, p],
            device_id={"filt": g}, device_id_type=MESH)

    for p in range(2):
        for g in peers:
            gather(g, p).start()
    ra[f] = xs[quarter]

    def halo(ref, send, recv, kind, i):
        m = 2 * kind + i
        across = 2 * kind + 1 - i
        if kind == NEAR:
            valid, to, step = None, m, (0, -outward)
            edge, there, here = (1 + i, near_edge), (1 + i, 3 * core), (1 + i, near_halo)
        elif kind == FAR:
            valid, to, step = has_far, m, (0, outward)
            edge, there, here = (1 + i, far_edge), (1 + i, 3 - 3 * core), (1 + i, far_halo)
        elif kind == FACE:
            valid, to, step = has_depth(i), across, (2 * i - 1, 0)
            edge, there, here = (1 + i, near_edge), (3 - 3 * i, near_edge), (3 * i, near_edge)
        elif kind == REST:
            valid, to, step = has_depth(i), across, (2 * i - 1, 0)
            edge, there, here = (1 + i, far_edge), (3 - 3 * i, far_edge), (3 * i, far_edge)
        elif kind == CORNER:
            valid, to, step = has_depth(i) & has_far, across, (2 * i - 1, outward)
            edge, there, here = (1 + i, far_edge), (3 - 3 * i, 3 - 3 * core), (3 * i, far_halo)
        else:
            valid, to, step = has_depth(i), m, (0, -outward)
            edge, there, here = (3 * i, near_edge), (3 * i, 3 * core), (3 * i, near_halo)
        _, device = neighbour(*step)

        def copy():
            return pltpu.make_async_remote_copy(
                src_ref=ref.at[edge], dst_ref=ref.at[there],
                send_sem=send.at[m], recv_sem=recv.at[to],
                device_id=device, device_id_type=MESH)

        def arrival():
            return pltpu.make_async_remote_copy(
                src_ref=ref.at[edge], dst_ref=ref.at[here],
                send_sem=send.at[m], recv_sem=recv.at[m],
                device_id=device, device_id_type=MESH)

        return valid, copy, arrival

    def when(valid, act):
        if valid is None:
            act()
        else:
            pl.when(valid)(act)

    def start(refs, i, *kinds):
        for kind in kinds:
            valid, copy, _ = halo(*refs, kind, i)
            when(valid, lambda: copy().start())

    def finish(refs, i, *kinds):
        for kind in kinds:
            valid, _, arrival = halo(*refs, kind, i)
            when(valid, lambda: arrival().wait_recv())

    def forward(refs, i):
        valid, _, arrival = halo(*refs, FACE, i)
        _, copy, _ = halo(*refs, FORWARD, i)

        @pl.when(valid)
        def _():
            arrival().wait_recv()
            copy().start()

    sends = (FACE, FAR, CORNER, REST, NEAR)
    first, second = (xh, sb, qb), (hh, sc, qc)
    for p, row in enumerate(order):
        for g in reversed(peers):
            gathered(g, p).wait_recv()
        for j in range(2):
            xh[1 + row, 1 + j] = jnp.concatenate(
                [ra[g, row, :, j * shard : (j + 1) * shard] for g in range(4)], axis=-1)
        start(first, row, *sends)
    loads[1].wait()
    loads[3].wait()
    for row in order:
        forward(first, row)
    for row in order:
        finish(first, row, NEAR, FAR)
    inner_taps(xh, w1, acc)
    for row in order:
        finish(first, row, FORWARD, CORNER, REST)
        hh[1 + row, 1:3] = outer_taps(xh, w1, acc, bb1, row).reshape(2, width, 4 * shard)
        start(second, row, *sends)

    loads[2].wait()
    loads[4].wait()
    for row in order:
        forward(second, row)
    for row in order:
        finish(second, row, NEAR, FAR)
    inner_taps(hh, w2, acc)

    def scatter(g, row):
        return pltpu.make_async_remote_copy(
            src_ref=os.at[g, row], dst_ref=ro.at[quarter, row],
            send_sem=se.at[g, row], recv_sem=qe.at[quarter, row],
            device_id={"filt": g}, device_id_type=MESH)

    def scattered(g, row):
        q = quarter_of(g)
        return pltpu.make_async_remote_copy(
            src_ref=os.at[g, row], dst_ref=ro.at[q, row],
            send_sem=se.at[g, row], recv_sem=qe.at[q, row],
            device_id={"filt": g}, device_id_type=MESH)

    for row in order:
        finish(second, row, FORWARD, CORNER, REST)
        result = outer_taps(hh, w2, acc, bb2, row)
        for g in range(4):
            part = result[:, g * shard : (g + 1) * shard]
            os[g, row] = jnp.concatenate([part[:width], part[width:]], axis=-1)
        for g in peers:
            scatter(g, row).start()
        ro[quarter, row] = os[f, row]

    for g in peers:
        for p in range(2):
            gather(g, p).wait_send()
    for refs in (first, second):
        for kind in range(6):
            for i in range(2):
                valid, copy, _ = halo(*refs, kind, i)
                when(valid, lambda: copy().wait_send())

    for row in range(2):
        for g in reversed(peers):
            scattered(g, row).wait_recv()
        for q in range(4):
            for j in range(2):
                out[2 * (q // 2) + row, 2 * (q % 2) + j] = ro[q, row, :, j * shard : (j + 1) * shard]
    for row in range(2):
        for g in peers:
            scatter(g, row).wait_send()


def body(depths, heights, volume, kernel_one, bias_one, kernel_two, bias_two):
    _, _, width, shard = volume.shape
    chans = 4 * shard
    bf16, dma = jnp.bfloat16, pltpu.SemaphoreType.DMA
    packed = pltpu.VMEM((4, 2, width, 2 * shard), bf16)
    padded = pltpu.VMEM((4, 4, width, chans), bf16)
    bias = pltpu.VMEM((1, chans), jnp.float32)
    return pl.pallas_call(
        functools.partial(kernel, depths, heights),
        out_shape=jax.ShapeDtypeStruct(volume.shape, bf16),
        in_specs=[pl.BlockSpec(memory_space=pltpu.HBM)] * 5,
        out_specs=pl.BlockSpec(memory_space=pltpu.VMEM),
        scratch_shapes=[
            pltpu.VMEM(volume.shape, bf16),
            pltpu.VMEM(kernel_one.shape, bf16),
            pltpu.VMEM(kernel_two.shape, bf16),
            bias,
            bias,
            packed,
            packed,
            padded,
            padded,
            packed,
            packed,
            pltpu.VMEM((3, 2, 2 * width, chans), jnp.float32),
            dma((5,)), dma((4, 2)), dma((4, 2)), dma((12,)), dma((12,)), dma((12,)), dma((12,)), dma((4, 2)), dma((4, 2)),
        ],
        compiler_params=pltpu.CompilerParams(
            collective_id=0, has_side_effects=True, vmem_limit_bytes=VMEM_LIMIT),
    )(*(pltpu.with_memory_space_constraint(v, pltpu.HBM) for v in (volume, kernel_one, bias_one.reshape(1, chans), kernel_two, bias_two.reshape(1, chans))))


def solution(mesh):
    in_specs = (P("depth", "height", None, "filt"), P(), P(), P(), P())
    out_specs = P("depth", "height", None, "filt")
    step = functools.partial(body, mesh.shape["depth"], mesh.shape["height"])
    return jax.shard_map(step, mesh=mesh, in_specs=in_specs, out_specs=out_specs, check_vma=False)
```

```python
import functools

import jax
import jax.numpy as jnp
from jax import lax
from jax.experimental import pallas as pl
from jax.experimental.pallas import tpu as pltpu
from jax.sharding import PartitionSpec as P

MESH = pl.DeviceIdType.MESH
VMEM_LIMIT = 40_000_000
STEPS = tuple((a, b) for a in (-1, 0, 1) for b in (-1, 0, 1) if (a, b) != (0, 0))
NEAR, FAR, FACE, REST, CORNER, FORWARD = (range(2 * i, 2 * i + 2) for i in range(6))


def flip_of(d):
    return (d % 2) * (1 - (d % 4) // 2)


def leaky(value):
    return jnp.where(value > 0, value, 0.3 * value)


def taps(x, w, rows, count, a, c):
    width, chans = x.shape[2], x.shape[3]
    total = None
    for b in range(3):
        lhs = x[rows : rows + count, b : b + 2].reshape(count * 2 * width, chans)
        part = jnp.dot(lhs, w[a, b, c], preferred_element_type=jnp.float32)
        total = part if total is None else total + part
    return total


def inner_taps(x, w, acc):
    half = 2 * x.shape[2]
    for c in range(3):
        both = taps(x, w, 1, 2, 1, c)
        acc[c, 0] = both[:half] + taps(x, w, 2, 1, 2, c)
        acc[c, 1] = both[half:] + taps(x, w, 1, 1, 0, c)


def outer_taps(x, w, acc, bias, row):
    width, chans = x.shape[2], x.shape[3]
    rows = 2 * width
    low, centre, high = (acc[c, row] + taps(x, w, 3 * row, 1, 2 * row, c) for c in range(3))
    w_of = lax.rem(lax.broadcasted_iota(jnp.int32, (rows, chans), 0), width)
    low = jnp.where(w_of == 0, 0.0, pltpu.roll(low, 1, 0))
    high = jnp.where(w_of == width - 1, 0.0, pltpu.roll(high, rows - 1, 0))
    return leaky(low + centre + high + bias[...]).astype(jnp.bfloat16)


def kernel(
    depths, heights,
    vol, k1, b1, k2, b2, out,
    xv, w1, w2, bb1, bb2, xs, ra, xh, hh, os, ro, acc,
    lsem, sa, qa, sb, qb, sc, qc, se, qe,
):
    d, h, f = lax.axis_index("depth"), lax.axis_index("height"), lax.axis_index("filt")
    flip = flip_of(d)
    width, shard = vol.shape[2], vol.shape[3]

    def quarter_of(g):
        return 2 * ((g // 2 + flip) % 2) + g % 2

    quarter = quarter_of(f)
    peers = [(f + r) % 4 for r in (2, 3, 1)]
    fine_d, fine_h = 2 * d + quarter // 2, 2 * h + f % 2
    def neighbour(sd, sh):
        nd, nh = fine_d + sd, fine_h + sh
        block = nd // 2
        nf = 2 * ((nd + flip_of(block)) % 2) + nh % 2
        valid = (nd >= 0) & (nd < 2 * depths) & (nh >= 0) & (nh < 2 * heights)
        return valid, {"depth": block, "height": nh // 2, "filt": nf}

    loads = [
        pltpu.make_async_copy(src, dst, lsem.at[i])
        for i, (src, dst) in enumerate(((vol, xv), (b1, bb1), (b2, bb2), (k1, w1), (k2, w2)))
    ]
    loads[0].start()
    barrier = pltpu.get_barrier_semaphore()
    for step in STEPS:
        valid, device = neighbour(*step)

        @pl.when(valid)
        def _():
            pl.semaphore_signal(barrier, inc=1, device_id=device, device_id_type=MESH)

    for load in loads[1:]:
        load.start()
    loads[0].wait()
    for q in range(4):
        top, side = 2 * (q // 2), 2 * (q % 2)
        xs[q] = jnp.concatenate([xv[top : top + 2, side], xv[top : top + 2, side + 1]], axis=-1)

    core = f % 2
    outward = 2 * core - 1
    near_edge, near_halo = 2 - core, 3 - 3 * core
    far_edge, far_halo = 1 + core, 3 * core
    has_far = (fine_h + outward >= 0) & (fine_h + outward < 2 * heights)
    has_depth = (fine_d > 0, fine_d < 2 * depths - 1)

    for ref in (xh, hh):
        @pl.when(jnp.logical_not(has_far))
        def _():
            for row in range(4):
                ref[row, far_halo] = jnp.zeros_like(ref[row, far_halo])

        for i in range(2):
            @pl.when(jnp.logical_not(has_depth[i]))
            def _():
                ref[3 * i] = jnp.zeros_like(ref[3 * i])

    tall = 3 - jnp.where(fine_d == 0, 1, 0) - jnp.where(fine_d == 2 * depths - 1, 1, 0)
    wide = 3 - jnp.where(fine_h == 0, 1, 0) - jnp.where(fine_h == 2 * heights - 1, 1, 0)
    pl.semaphore_wait(barrier, tall * wide - 1)

    def gather(g):
        return pltpu.make_async_remote_copy(
            src_ref=xs.at[quarter_of(g)], dst_ref=ra.at[f], send_sem=sa.at[g], recv_sem=qa.at[f],
            device_id={"filt": g}, device_id_type=MESH)

    def gathered(g):
        return pltpu.make_async_remote_copy(
            src_ref=xs.at[quarter], dst_ref=ra.at[g], send_sem=sa.at[g], recv_sem=qa.at[g],
            device_id={"filt": g}, device_id_type=MESH)

    for g in peers:
        gather(g).start()
    ra[f] = xs[quarter]
    for g in reversed(peers):
        gathered(g).wait_recv()
    for i in range(2):
        for j in range(2):
            xh[1 + i, 1 + j] = jnp.concatenate(
                [ra[g, i, :, j * shard : (j + 1) * shard] for g in range(4)], axis=-1)

    def halo(ref, send, recv, m):
        i = m % 2
        if m in NEAR:
            valid, to, step = None, m, (0, -outward)
            edge, there, here = (1 + i, near_edge), (1 + i, 3 * core), (1 + i, near_halo)
        elif m in FAR:
            valid, to, step = has_far, m, (0, outward)
            edge, there, here = (1 + i, far_edge), (1 + i, 3 - 3 * core), (1 + i, far_halo)
        elif m in FACE:
            valid, to, step = has_depth[i], FACE[1 - i], (2 * i - 1, 0)
            edge, there, here = (1 + i, near_edge), (3 - 3 * i, near_edge), (3 * i, near_edge)
        elif m in REST:
            valid, to, step = has_depth[i], REST[1 - i], (2 * i - 1, 0)
            edge, there, here = (1 + i, far_edge), (3 - 3 * i, far_edge), (3 * i, far_edge)
        elif m in CORNER:
            valid, to, step = has_depth[i] & has_far, CORNER[1 - i], (2 * i - 1, outward)
            edge, there, here = (1 + i, far_edge), (3 - 3 * i, 3 - 3 * core), (3 * i, far_halo)
        else:
            valid, to, step = has_depth[i], m, (0, -outward)
            edge, there, here = (3 * i, near_edge), (3 * i, 3 * core), (3 * i, near_halo)
        _, device = neighbour(*step)

        def copy():
            return pltpu.make_async_remote_copy(
                src_ref=ref.at[edge], dst_ref=ref.at[there],
                send_sem=send.at[m], recv_sem=recv.at[to],
                device_id=device, device_id_type=MESH)

        def arrival():
            return pltpu.make_async_remote_copy(
                src_ref=ref.at[edge], dst_ref=ref.at[here],
                send_sem=send.at[m], recv_sem=recv.at[m],
                device_id=device, device_id_type=MESH)

        return valid, copy, arrival

    def when(valid, act):
        if valid is None:
            act()
        else:
            pl.when(valid)(act)

    def start(refs, *messages):
        for m in messages:
            valid, copy, _ = halo(*refs, m)
            when(valid, lambda: copy().start())

    def finish(refs, *messages):
        for m in messages:
            valid, _, arrival = halo(*refs, m)
            when(valid, lambda: arrival().wait_recv())

    def forward(refs, i):
        valid, _, arrival = halo(*refs, FACE[i])
        _, copy, _ = halo(*refs, FORWARD[i])

        @pl.when(valid)
        def _():
            arrival().wait_recv()
            copy().start()

    first, second = (xh, sb, qb), (hh, sc, qc)
    start(first, *FACE, *FAR, *CORNER, *REST, *NEAR)
    loads[1].wait()
    loads[3].wait()
    def scatter(g, row):
        return pltpu.make_async_remote_copy(
            src_ref=os.at[g, row], dst_ref=ro.at[quarter, row],
            send_sem=se.at[g, row], recv_sem=qe.at[quarter, row],
            device_id={"filt": g}, device_id_type=MESH)

    def scattered(g, row):
        q = quarter_of(g)
        return pltpu.make_async_remote_copy(
            src_ref=os.at[g, row], dst_ref=ro.at[q, row],
            send_sem=se.at[g, row], recv_sem=qe.at[q, row],
            device_id={"filt": g}, device_id_type=MESH)

    def both(order):
        for row in order:
            forward(first, row)
        finish(first, *NEAR, *FAR)
        inner_taps(xh, w1, acc)
        for row in order:
            finish(first, FORWARD[row], CORNER[row], REST[row])
            hh[1 + row, 1:3] = outer_taps(xh, w1, acc, bb1, row).reshape(2, width, 4 * shard)
            start(second, FACE[row], FAR[row], CORNER[row], REST[row], NEAR[row])

        loads[2].wait()
        loads[4].wait()
        for row in order:
            forward(second, row)
        finish(second, *NEAR, *FAR)
        inner_taps(hh, w2, acc)

        for row in order:
            finish(second, FORWARD[row], CORNER[row], REST[row])
            result = outer_taps(hh, w2, acc, bb2, row)
            for g in range(4):
                part = result[:, g * shard : (g + 1) * shard]
                os[g, row] = jnp.concatenate([part[:width], part[width:]], axis=-1)
            for g in peers:
                scatter(g, row).start()
            ro[quarter, row] = os[f, row]

    @pl.when(quarter // 2 == 0)
    def _():
        both((1, 0))

    @pl.when(quarter // 2 == 1)
    def _():
        both((0, 1))

    for g in peers:
        gather(g).wait_send()
    for refs in (first, second):
        for m in range(12):
            valid, copy, _ = halo(*refs, m)
            when(valid, lambda: copy().wait_send())

    for row in range(2):
        for g in reversed(peers):
            scattered(g, row).wait_recv()
        for q in range(4):
            for j in range(2):
                out[2 * (q // 2) + row, 2 * (q % 2) + j] = ro[q, row, :, j * shard : (j + 1) * shard]
    for row in range(2):
        for g in peers:
            scatter(g, row).wait_send()


def body(depths, heights, volume, kernel_one, bias_one, kernel_two, bias_two):
    _, _, width, shard = volume.shape
    chans = 4 * shard
    bf16, dma = jnp.bfloat16, pltpu.SemaphoreType.DMA
    packed = pltpu.VMEM((4, 2, width, 2 * shard), bf16)
    padded = pltpu.VMEM((4, 4, width, chans), bf16)
    bias = pltpu.VMEM((1, chans), jnp.float32)
    return pl.pallas_call(
        functools.partial(kernel, depths, heights),
        out_shape=jax.ShapeDtypeStruct(volume.shape, bf16),
        in_specs=[pl.BlockSpec(memory_space=pltpu.HBM)] * 5,
        out_specs=pl.BlockSpec(memory_space=pltpu.VMEM),
        scratch_shapes=[
            pltpu.VMEM(volume.shape, bf16),
            pltpu.VMEM(kernel_one.shape, bf16),
            pltpu.VMEM(kernel_two.shape, bf16),
            bias,
            bias,
            packed,
            packed,
            padded,
            padded,
            packed,
            packed,
            pltpu.VMEM((3, 2, 2 * width, chans), jnp.float32),
            dma((5,)), dma((4,)), dma((4,)), dma((12,)), dma((12,)), dma((12,)), dma((12,)), dma((4, 2)), dma((4, 2)),
        ],
        compiler_params=pltpu.CompilerParams(
            collective_id=0, has_side_effects=True, vmem_limit_bytes=VMEM_LIMIT),
    )(*(pltpu.with_memory_space_constraint(v, pltpu.HBM) for v in (volume, kernel_one, bias_one.reshape(1, chans), kernel_two, bias_two.reshape(1, chans))))


def solution(mesh):
    in_specs = (P("depth", "height", None, "filt"), P(), P(), P(), P())
    out_specs = P("depth", "height", None, "filt")
    step = functools.partial(body, mesh.shape["depth"], mesh.shape["height"])
    return jax.shard_map(step, mesh=mesh, in_specs=in_specs, out_specs=out_specs, check_vma=False)
```

```python
import functools

import jax
import jax.numpy as jnp
from jax import lax
from jax.experimental import pallas as pl
from jax.experimental.pallas import tpu as pltpu
from jax.sharding import PartitionSpec as P

MESH = pl.DeviceIdType.MESH
VMEM_LIMIT = 40_000_000
STEPS = tuple((a, b) for a in (-1, 0, 1) for b in (-1, 0, 1) if (a, b) != (0, 0))
NEAR, FAR, FACE, REST, CORNER, INNER = (range(2 * i, 2 * i + 2) for i in range(6))


def flip_of(d):
    return (d % 2) * (1 - (d % 4) // 2)


def leaky(value):
    return jnp.where(value > 0, value, 0.3 * value)


def taps(x, w, rows, count, a, c):
    width, chans = x.shape[2], x.shape[3]
    total = None
    for b in range(3):
        lhs = x[rows : rows + count, b : b + 2].reshape(count * 2 * width, chans)
        part = jnp.dot(lhs, w[a, b, c], preferred_element_type=jnp.float32)
        total = part if total is None else total + part
    return total


def inner_taps(x, w, acc):
    half = 2 * x.shape[2]
    for c in range(3):
        both = taps(x, w, 1, 2, 1, c)
        acc[c, 0] = both[:half] + taps(x, w, 2, 1, 2, c)
        acc[c, 1] = both[half:] + taps(x, w, 1, 1, 0, c)


def outer_taps(x, w, acc, bias, row):
    width, chans = x.shape[2], x.shape[3]
    rows = 2 * width
    low, centre, high = (acc[c, row] + taps(x, w, 3 * row, 1, 2 * row, c) for c in range(3))
    w_of = lax.rem(lax.broadcasted_iota(jnp.int32, (rows, chans), 0), width)
    low = jnp.where(w_of == 0, 0.0, pltpu.roll(low, 1, 0))
    high = jnp.where(w_of == width - 1, 0.0, pltpu.roll(high, rows - 1, 0))
    return leaky(low + centre + high + bias[...]).astype(jnp.bfloat16)


def kernel(
    depths, heights,
    vol, k1, b1, k2, b2, out,
    xv, w1, w2, bb1, bb2, xs, ra, xh, hh, os, ro, acc,
    lsem, sa, qa, sb, qb, sc, qc, se, qe,
):
    d, h, f = lax.axis_index("depth"), lax.axis_index("height"), lax.axis_index("filt")
    flip = flip_of(d)
    width, shard = vol.shape[2], vol.shape[3]

    def quarter_of(g):
        return 2 * ((g // 2 + flip) % 2) + g % 2

    quarter = quarter_of(f)
    peers = [(f + r) % 4 for r in (2, 3, 1)]
    fine_d, fine_h = 2 * d + quarter // 2, 2 * h + f % 2
    def neighbour(sd, sh):
        nd, nh = fine_d + sd, fine_h + sh
        block = nd // 2
        nf = 2 * ((nd + flip_of(block)) % 2) + nh % 2
        valid = (nd >= 0) & (nd < 2 * depths) & (nh >= 0) & (nh < 2 * heights)
        return valid, {"depth": block, "height": nh // 2, "filt": nf}

    loads = [
        pltpu.make_async_copy(src, dst, lsem.at[i])
        for i, (src, dst) in enumerate(((vol, xv), (b1, bb1), (b2, bb2), (k1, w1), (k2, w2)))
    ]
    loads[0].start()
    barrier = pltpu.get_barrier_semaphore()
    for step in STEPS:
        valid, device = neighbour(*step)

        @pl.when(valid)
        def _():
            pl.semaphore_signal(barrier, inc=1, device_id=device, device_id_type=MESH)

    for load in loads[1:]:
        load.start()
    loads[0].wait()
    for q in range(4):
        top, side = 2 * (q // 2), 2 * (q % 2)
        xs[q] = jnp.concatenate([xv[top : top + 2, side], xv[top : top + 2, side + 1]], axis=-1)

    core = f % 2
    outward = 2 * core - 1
    near_edge, near_halo = 2 - core, 3 - 3 * core
    far_edge, far_halo = 1 + core, 3 * core
    has_far = (fine_h + outward >= 0) & (fine_h + outward < 2 * heights)
    has_depth = (fine_d > 0, fine_d < 2 * depths - 1)

    for ref in (xh, hh):
        @pl.when(jnp.logical_not(has_far))
        def _():
            for row in range(4):
                ref[row, far_halo] = jnp.zeros_like(ref[row, far_halo])

        for i in range(2):
            @pl.when(jnp.logical_not(has_depth[i]))
            def _():
                ref[3 * i] = jnp.zeros_like(ref[3 * i])

    tall = 3 - jnp.where(fine_d == 0, 1, 0) - jnp.where(fine_d == 2 * depths - 1, 1, 0)
    wide = 3 - jnp.where(fine_h == 0, 1, 0) - jnp.where(fine_h == 2 * heights - 1, 1, 0)
    pl.semaphore_wait(barrier, tall * wide - 1)

    def gather(g):
        return pltpu.make_async_remote_copy(
            src_ref=xs.at[quarter_of(g)], dst_ref=ra.at[f], send_sem=sa.at[g], recv_sem=qa.at[f],
            device_id={"filt": g}, device_id_type=MESH)

    def gathered(g):
        return pltpu.make_async_remote_copy(
            src_ref=xs.at[quarter], dst_ref=ra.at[g], send_sem=sa.at[g], recv_sem=qa.at[g],
            device_id={"filt": g}, device_id_type=MESH)

    for g in peers:
        gather(g).start()
    ra[f] = xs[quarter]
    for g in reversed(peers):
        gathered(g).wait_recv()
    for i in range(2):
        for j in range(2):
            xh[1 + i, 1 + j] = jnp.concatenate(
                [ra[g, i, :, j * shard : (j + 1) * shard] for g in range(4)], axis=-1)

    def halo(ref, send, recv, m):
        i = m % 2
        if m in NEAR:
            valid, to, step = None, m, (0, -outward)
            edge, there, here = (1 + i, near_edge), (1 + i, 3 * core), (1 + i, near_halo)
        elif m in FAR:
            valid, to, step = has_far, m, (0, outward)
            edge, there, here = (1 + i, far_edge), (1 + i, 3 - 3 * core), (1 + i, far_halo)
        elif m in FACE:
            valid, to, step = has_depth[i], FACE[1 - i], (2 * i - 1, 0)
            edge, there, here = (1 + i, near_edge), (3 - 3 * i, near_edge), (3 * i, near_edge)
        elif m in REST:
            valid, to, step = has_depth[i], REST[1 - i], (2 * i - 1, 0)
            edge, there, here = (1 + i, far_edge), (3 - 3 * i, far_edge), (3 * i, far_edge)
        elif m in CORNER:
            valid, to, step = has_depth[i] & has_far, CORNER[1 - i], (2 * i - 1, outward)
            edge, there, here = (1 + i, far_edge), (3 - 3 * i, 3 - 3 * core), (3 * i, far_halo)
        else:
            valid, to, step = has_depth[i], INNER[1 - i], (2 * i - 1, -outward)
            edge, there, here = (1 + i, near_edge), (3 - 3 * i, 3 * core), (3 * i, near_halo)
        _, device = neighbour(*step)

        def copy():
            return pltpu.make_async_remote_copy(
                src_ref=ref.at[edge], dst_ref=ref.at[there],
                send_sem=send.at[m], recv_sem=recv.at[to],
                device_id=device, device_id_type=MESH)

        def arrival():
            return pltpu.make_async_remote_copy(
                src_ref=ref.at[edge], dst_ref=ref.at[here],
                send_sem=send.at[m], recv_sem=recv.at[m],
                device_id=device, device_id_type=MESH)

        return valid, copy, arrival

    def when(valid, act):
        if valid is None:
            act()
        else:
            pl.when(valid)(act)

    def start(refs, *messages):
        for m in messages:
            valid, copy, _ = halo(*refs, m)
            when(valid, lambda: copy().start())

    def finish(refs, *messages):
        for m in messages:
            valid, _, arrival = halo(*refs, m)
            when(valid, lambda: arrival().wait_recv())

    first, second = (xh, sb, qb), (hh, sc, qc)
    start(first, *CORNER, *FAR, *INNER, *FACE, *REST, *NEAR)
    loads[1].wait()
    loads[3].wait()
    finish(first, *NEAR, *FAR)
    inner_taps(xh, w1, acc)
    for row in range(2):
        finish(first, CORNER[row], INNER[row], FACE[row], REST[row])
        hh[1 + row, 1:3] = outer_taps(xh, w1, acc, bb1, row).reshape(2, width, 4 * shard)
        start(second, CORNER[row], FAR[row], INNER[row], FACE[row], REST[row], NEAR[row])

    loads[2].wait()
    loads[4].wait()
    finish(second, *NEAR, *FAR)
    inner_taps(hh, w2, acc)

    def scatter(g, row):
        return pltpu.make_async_remote_copy(
            src_ref=os.at[g, row], dst_ref=ro.at[quarter, row],
            send_sem=se.at[g, row], recv_sem=qe.at[quarter, row],
            device_id={"filt": g}, device_id_type=MESH)

    def scattered(g, row):
        q = quarter_of(g)
        return pltpu.make_async_remote_copy(
            src_ref=os.at[g, row], dst_ref=ro.at[q, row],
            send_sem=se.at[g, row], recv_sem=qe.at[q, row],
            device_id={"filt": g}, device_id_type=MESH)

    for row in range(2):
        finish(second, CORNER[row], INNER[row], FACE[row], REST[row])
        result = outer_taps(hh, w2, acc, bb2, row)
        for g in range(4):
            part = result[:, g * shard : (g + 1) * shard]
            os[g, row] = jnp.concatenate([part[:width], part[width:]], axis=-1)
        for g in peers:
            scatter(g, row).start()
        ro[quarter, row] = os[f, row]

    for g in peers:
        gather(g).wait_send()
    for refs in (first, second):
        for m in range(12):
            valid, copy, _ = halo(*refs, m)
            when(valid, lambda: copy().wait_send())

    for row in range(2):
        for g in reversed(peers):
            scattered(g, row).wait_recv()
        for q in range(4):
            for j in range(2):
                out[2 * (q // 2) + row, 2 * (q % 2) + j] = ro[q, row, :, j * shard : (j + 1) * shard]
    for row in range(2):
        for g in peers:
            scatter(g, row).wait_send()


def body(depths, heights, volume, kernel_one, bias_one, kernel_two, bias_two):
    _, _, width, shard = volume.shape
    chans = 4 * shard
    bf16, dma = jnp.bfloat16, pltpu.SemaphoreType.DMA
    packed = pltpu.VMEM((4, 2, width, 2 * shard), bf16)
    padded = pltpu.VMEM((4, 4, width, chans), bf16)
    bias = pltpu.VMEM((1, chans), jnp.float32)
    return pl.pallas_call(
        functools.partial(kernel, depths, heights),
        out_shape=jax.ShapeDtypeStruct(volume.shape, bf16),
        in_specs=[pl.BlockSpec(memory_space=pltpu.HBM)] * 5,
        out_specs=pl.BlockSpec(memory_space=pltpu.VMEM),
        scratch_shapes=[
            pltpu.VMEM(volume.shape, bf16),
            pltpu.VMEM(kernel_one.shape, bf16),
            pltpu.VMEM(kernel_two.shape, bf16),
            bias,
            bias,
            packed,
            packed,
            padded,
            padded,
            packed,
            packed,
            pltpu.VMEM((3, 2, 2 * width, chans), jnp.float32),
            dma((5,)), dma((4,)), dma((4,)), dma((12,)), dma((12,)), dma((12,)), dma((12,)), dma((4, 2)), dma((4, 2)),
        ],
        compiler_params=pltpu.CompilerParams(
            collective_id=0, has_side_effects=True, vmem_limit_bytes=VMEM_LIMIT),
    )(*(pltpu.with_memory_space_constraint(v, pltpu.HBM) for v in (volume, kernel_one, bias_one.reshape(1, chans), kernel_two, bias_two.reshape(1, chans))))


def solution(mesh):
    in_specs = (P("depth", "height", None, "filt"), P(), P(), P(), P())
    out_specs = P("depth", "height", None, "filt")
    step = functools.partial(body, mesh.shape["depth"], mesh.shape["height"])
    return jax.shard_map(step, mesh=mesh, in_specs=in_specs, out_specs=out_specs, check_vma=False)
```

```python
import functools

import jax
import jax.numpy as jnp
from jax import lax
from jax.experimental import pallas as pl
from jax.experimental.pallas import tpu as pltpu
from jax.sharding import PartitionSpec as P

MESH = pl.DeviceIdType.MESH
VMEM_LIMIT = 40_000_000
STEPS = tuple((a, b) for a in (-1, 0, 1) for b in (-1, 0, 1) if (a, b) != (0, 0))
NEAR, FAR, FACE, REST, CORNER, FORWARD = (range(2 * i, 2 * i + 2) for i in range(6))


def flip_of(d):
    return (d % 2) * (1 - (d % 4) // 2)


def leaky(value):
    return jnp.where(value > 0, value, 0.3 * value)


def taps(x, w, rows, count, a, c):
    width, chans = x.shape[2], x.shape[3]
    total = None
    for b in range(3):
        lhs = x[rows : rows + count, b : b + 2].reshape(count * 2 * width, chans)
        part = jnp.dot(lhs, w[a, b, c], preferred_element_type=jnp.float32)
        total = part if total is None else total + part
    return total


def inner_taps(x, w, acc):
    half = 2 * x.shape[2]
    for c in range(3):
        both = taps(x, w, 1, 2, 1, c)
        acc[c, 0] = both[:half] + taps(x, w, 2, 1, 2, c)
        acc[c, 1] = both[half:] + taps(x, w, 1, 1, 0, c)


def outer_taps(x, w, acc, bias, row):
    width, chans = x.shape[2], x.shape[3]
    rows = 2 * width
    low, centre, high = (acc[c, row] + taps(x, w, 3 * row, 1, 2 * row, c) for c in range(3))
    w_of = lax.rem(lax.broadcasted_iota(jnp.int32, (rows, chans), 0), width)
    low = jnp.where(w_of == 0, 0.0, pltpu.roll(low, 1, 0))
    high = jnp.where(w_of == width - 1, 0.0, pltpu.roll(high, rows - 1, 0))
    return leaky(low + centre + high + bias[...]).astype(jnp.bfloat16)


def kernel(
    depths, heights,
    vol, k1, b1, k2, b2, out,
    xv, w1, w2, bb1, bb2, xs, ra, xh, hh, os, ro, acc,
    lsem, sa, qa, sb, qb, sc, qc, se, qe,
):
    d, h, f = lax.axis_index("depth"), lax.axis_index("height"), lax.axis_index("filt")
    flip = flip_of(d)
    width, shard = vol.shape[2], vol.shape[3]

    def quarter_of(g):
        return 2 * ((g // 2 + flip) % 2) + g % 2

    quarter = quarter_of(f)
    peers = [(f + r) % 4 for r in (2, 3, 1)]
    fine_d, fine_h = 2 * d + quarter // 2, 2 * h + f % 2
    def neighbour(sd, sh):
        nd, nh = fine_d + sd, fine_h + sh
        block = nd // 2
        nf = 2 * ((nd + flip_of(block)) % 2) + nh % 2
        valid = (nd >= 0) & (nd < 2 * depths) & (nh >= 0) & (nh < 2 * heights)
        return valid, {"depth": block, "height": nh // 2, "filt": nf}

    loads = [
        pltpu.make_async_copy(src, dst, lsem.at[i])
        for i, (src, dst) in enumerate(((vol, xv), (b1, bb1), (b2, bb2), (k1, w1), (k2, w2)))
    ]
    loads[0].start()
    barrier = pltpu.get_barrier_semaphore()
    for step in STEPS:
        valid, device = neighbour(*step)

        @pl.when(valid)
        def _():
            pl.semaphore_signal(barrier, inc=1, device_id=device, device_id_type=MESH)

    for load in loads[1:]:
        load.start()
    loads[0].wait()
    for q in range(4):
        top, side = 2 * (q // 2), 2 * (q % 2)
        xs[q] = jnp.concatenate([xv[top : top + 2, side], xv[top : top + 2, side + 1]], axis=-1)

    core = f % 2
    outward = 2 * core - 1
    near_edge, near_halo = 2 - core, 3 - 3 * core
    far_edge, far_halo = 1 + core, 3 * core
    has_far = (fine_h + outward >= 0) & (fine_h + outward < 2 * heights)
    has_depth = (fine_d > 0, fine_d < 2 * depths - 1)

    for ref in (xh, hh):
        @pl.when(jnp.logical_not(has_far))
        def _():
            for row in range(4):
                ref[row, far_halo] = jnp.zeros_like(ref[row, far_halo])

        for i in range(2):
            @pl.when(jnp.logical_not(has_depth[i]))
            def _():
                ref[3 * i] = jnp.zeros_like(ref[3 * i])

    tall = 3 - jnp.where(fine_d == 0, 1, 0) - jnp.where(fine_d == 2 * depths - 1, 1, 0)
    wide = 3 - jnp.where(fine_h == 0, 1, 0) - jnp.where(fine_h == 2 * heights - 1, 1, 0)
    pl.semaphore_wait(barrier, tall * wide - 1)

    def gather(g):
        return pltpu.make_async_remote_copy(
            src_ref=xs.at[quarter_of(g)], dst_ref=ra.at[f], send_sem=sa.at[g], recv_sem=qa.at[f],
            device_id={"filt": g}, device_id_type=MESH)

    def gathered(g):
        return pltpu.make_async_remote_copy(
            src_ref=xs.at[quarter], dst_ref=ra.at[g], send_sem=sa.at[g], recv_sem=qa.at[g],
            device_id={"filt": g}, device_id_type=MESH)

    for g in peers:
        gather(g).start()
    ra[f] = xs[quarter]
    for g in reversed(peers):
        gathered(g).wait_recv()
    for i in range(2):
        for j in range(2):
            xh[1 + i, 1 + j] = jnp.concatenate(
                [ra[g, i, :, j * shard : (j + 1) * shard] for g in range(4)], axis=-1)

    def halo(ref, send, recv, m):
        i = m % 2
        if m in NEAR:
            valid, to, step = None, m, (0, -outward)
            edge, there, here = (1 + i, near_edge), (1 + i, 3 * core), (1 + i, near_halo)
        elif m in FAR:
            valid, to, step = has_far, m, (0, outward)
            edge, there, here = (1 + i, far_edge), (1 + i, 3 - 3 * core), (1 + i, far_halo)
        elif m in FACE:
            valid, to, step = has_depth[i], FACE[1 - i], (2 * i - 1, 0)
            edge, there, here = (1 + i, near_edge), (3 - 3 * i, near_edge), (3 * i, near_edge)
        elif m in REST:
            valid, to, step = has_depth[i], REST[1 - i], (2 * i - 1, 0)
            edge, there, here = (1 + i, far_edge), (3 - 3 * i, far_edge), (3 * i, far_edge)
        elif m in CORNER:
            valid, to, step = has_depth[i] & has_far, CORNER[1 - i], (2 * i - 1, outward)
            edge, there, here = (1 + i, far_edge), (3 - 3 * i, 3 - 3 * core), (3 * i, far_halo)
        else:
            valid, to, step = has_depth[i], m, (0, -outward)
            edge, there, here = (3 * i, near_edge), (3 * i, 3 * core), (3 * i, near_halo)
        _, device = neighbour(*step)

        def copy():
            return pltpu.make_async_remote_copy(
                src_ref=ref.at[edge], dst_ref=ref.at[there],
                send_sem=send.at[m], recv_sem=recv.at[to],
                device_id=device, device_id_type=MESH)

        def arrival():
            return pltpu.make_async_remote_copy(
                src_ref=ref.at[edge], dst_ref=ref.at[here],
                send_sem=send.at[m], recv_sem=recv.at[m],
                device_id=device, device_id_type=MESH)

        return valid, copy, arrival

    def when(valid, act):
        if valid is None:
            act()
        else:
            pl.when(valid)(act)

    def start(refs, *messages):
        for m in messages:
            valid, copy, _ = halo(*refs, m)
            when(valid, lambda: copy().start())

    def finish(refs, *messages):
        for m in messages:
            valid, _, arrival = halo(*refs, m)
            when(valid, lambda: arrival().wait_recv())

    def forward(refs, i):
        valid, _, arrival = halo(*refs, FACE[i])
        _, copy, _ = halo(*refs, FORWARD[i])

        @pl.when(valid)
        def _():
            arrival().wait_recv()
            copy().start()

    first, second = (xh, sb, qb), (hh, sc, qc)
    start(first, *FACE, *CORNER, *REST, *FAR, *NEAR)
    loads[1].wait()
    loads[3].wait()
    forward(first, 0)
    forward(first, 1)
    finish(first, *NEAR, *FAR)
    inner_taps(xh, w1, acc)
    for row in range(2):
        finish(first, FORWARD[row], CORNER[row], REST[row])
        hh[1 + row, 1:3] = outer_taps(xh, w1, acc, bb1, row).reshape(2, width, 4 * shard)
        start(second, FACE[row], CORNER[row], REST[row], FAR[row], NEAR[row])

    loads[2].wait()
    loads[4].wait()
    forward(second, 0)
    forward(second, 1)
    finish(second, *NEAR, *FAR)
    inner_taps(hh, w2, acc)

    def scatter(g, row):
        return pltpu.make_async_remote_copy(
            src_ref=os.at[g, row], dst_ref=ro.at[quarter, row],
            send_sem=se.at[g, row], recv_sem=qe.at[quarter, row],
            device_id={"filt": g}, device_id_type=MESH)

    def scattered(g, row):
        q = quarter_of(g)
        return pltpu.make_async_remote_copy(
            src_ref=os.at[g, row], dst_ref=ro.at[q, row],
            send_sem=se.at[g, row], recv_sem=qe.at[q, row],
            device_id={"filt": g}, device_id_type=MESH)

    for row in range(2):
        finish(second, FORWARD[row], CORNER[row], REST[row])
        result = outer_taps(hh, w2, acc, bb2, row)
        for g in range(4):
            part = result[:, g * shard : (g + 1) * shard]
            os[g, row] = jnp.concatenate([part[:width], part[width:]], axis=-1)
        for g in peers:
            scatter(g, row).start()
        ro[quarter, row] = os[f, row]

    for g in peers:
        gather(g).wait_send()
    for refs in (first, second):
        for m in range(12):
            valid, copy, _ = halo(*refs, m)
            when(valid, lambda: copy().wait_send())

    for row in range(2):
        for g in reversed(peers):
            scattered(g, row).wait_recv()
        for q in range(4):
            for j in range(2):
                out[2 * (q // 2) + row, 2 * (q % 2) + j] = ro[q, row, :, j * shard : (j + 1) * shard]
    for row in range(2):
        for g in peers:
            scatter(g, row).wait_send()


def body(depths, heights, volume, kernel_one, bias_one, kernel_two, bias_two):
    _, _, width, shard = volume.shape
    chans = 4 * shard
    bf16, dma = jnp.bfloat16, pltpu.SemaphoreType.DMA
    packed = pltpu.VMEM((4, 2, width, 2 * shard), bf16)
    padded = pltpu.VMEM((4, 4, width, chans), bf16)
    bias = pltpu.VMEM((1, chans), jnp.float32)
    return pl.pallas_call(
        functools.partial(kernel, depths, heights),
        out_shape=jax.ShapeDtypeStruct(volume.shape, bf16),
        in_specs=[pl.BlockSpec(memory_space=pltpu.HBM)] * 5,
        out_specs=pl.BlockSpec(memory_space=pltpu.VMEM),
        scratch_shapes=[
            pltpu.VMEM(volume.shape, bf16),
            pltpu.VMEM(kernel_one.shape, bf16),
            pltpu.VMEM(kernel_two.shape, bf16),
            bias,
            bias,
            packed,
            packed,
            padded,
            padded,
            packed,
            packed,
            pltpu.VMEM((3, 2, 2 * width, chans), jnp.float32),
            dma((5,)), dma((4,)), dma((4,)), dma((12,)), dma((12,)), dma((12,)), dma((12,)), dma((4, 2)), dma((4, 2)),
        ],
        compiler_params=pltpu.CompilerParams(
            collective_id=0, has_side_effects=True, vmem_limit_bytes=VMEM_LIMIT),
    )(*(pltpu.with_memory_space_constraint(v, pltpu.HBM) for v in (volume, kernel_one, bias_one.reshape(1, chans), kernel_two, bias_two.reshape(1, chans))))


def solution(mesh):
    in_specs = (P("depth", "height", None, "filt"), P(), P(), P(), P())
    out_specs = P("depth", "height", None, "filt")
    step = functools.partial(body, mesh.shape["depth"], mesh.shape["height"])
    return jax.shard_map(step, mesh=mesh, in_specs=in_specs, out_specs=out_specs, check_vma=False)
```
